256 devices in a mesh: cal: 2 (over x_lo), gr: 16 (over x_hi, y, core), gc: 8 (over z).
Axes of the slice: x: 4 (x_hi: 2, x_lo: 2; x = x_hi * 2 + x_lo), y: 4, z: 8, core: 2. Of those that a mesh axis runs over, the one named last changes fastest.
Arguments:
- tokens: bfloat16 [512, 8192], P(('gr', 'gc'), 'cal'), may hold values from -12 to 12
- gate_weight: bfloat16 [8192, 28672], P(None, ('cal', 'gr', 'gc')), may hold values from -0.0625 to 0.0625
- up_weight: bfloat16 [8192, 28672], P(None, ('cal', 'gr', 'gc')), may hold values from -0.0625 to 0.0625
- hessian_slab: float32 [28672, 8192], P(('cal', 'gr'), 'gc'), may hold values from -1.2 to 1.2
- weight_error: float32 [512, 28672], P(None, ('cal', 'gr')), may hold values from -0.18 to 0.18
- slab_offset: int32 [1], replicated, may hold values from 0 to 20480
- token_count: int32 [1], replicated, may hold values from 512 to 1023
Outputs:
- new_slab: float32 [28672, 8192], P(('cal', 'gr'), 'gc')
- gradient: float32 [512, 8192], P(('cal', 'gr'), 'gc')
The draws below stay inside these ranges and needn't reach their ends.
Inputs may be any that keep to these rules, and one draw needn't show every extreme that they name: The slab holds the Hessian's columns slab_offset[0] to slab_offset[0] + 8191.
All inputs are finite; a program needn't handle non-finite values.
Results may differ from the reference program's by a relative error of at most 0.0038.
Values may be sent and summed in bfloat16 or wider, within the bound.
No kernel may reach another device: no remote copies, remote signals or barrier semaphores. Data moves between devices by JAX's collectives and lax.ppermute only.
A program may use at most 64 MiB of HBM per device.

```python
import jax
import jax.numpy as jnp
from jax import lax

D = 8192
FF = 28672
SLAB = 8192
TOK = 512
ROWS = 512


def strengthened(values, key, source, target, parts, factor):
    owner, partner = [(jnp.arange(values.shape[axis_at]) // (values.shape[axis_at] // parts)).reshape([-1 if axis == axis_at else 1 for axis in range(values.ndim)]) for axis_at in (source, target)]
    chosen = jax.random.permutation(key, parts)[partner]
    strong = (owner == chosen) | (owner == (partner + parts // 2) % parts)
    return jnp.where(strong, factor * values, values)


def steps_of(rng, dims, pieces, smallest, largest):
    factor_of = 1.0
    for position, blocks in pieces:
        heights = jax.random.uniform(jax.random.fold_in(jax.random.fold_in(rng, 6), position), (blocks,), jnp.float32, smallest / len(pieces), largest / len(pieces))
        factor_of = factor_of * jnp.repeat(jnp.exp(heights), dims[position] // blocks).reshape((-1,) + (1,) * (len(dims) - 1 - position))
    return factor_of


def scatter_about(own_key, shape, spread, reach, cuts=(), dtype=jnp.bfloat16):
    entries = jax.random.normal(own_key, shape, jnp.float32) * spread
    if len(cuts) > 0:
        entries = steps_of(own_key, shape, cuts, -0.22, 0.18) * entries
    return jnp.clip(entries, min=-reach, max=reach).astype(dtype)


def heavy_noise(stream_key, dims, spread, limit, pieces, heavy, held_as=jnp.bfloat16):
    values = spread * jax.random.normal(stream_key, dims, jnp.float32)
    if pieces:
        values = values * steps_of(stream_key, dims, pieces, -0.22, 0.18)
    return jnp.clip(strengthened(values, jax.random.fold_in(stream_key, 3), *heavy), -limit, limit).astype(held_as)


def setup_inputs(seed: int = 0) -> dict:
    key_of = jax.random.split(jax.random.key(seed), 8)
    tokens = scatter_about(key_of[0], (TOK, D), 2.0, 12.0, ((0, 128), (1, 2)))
    gate_weight = scatter_about(key_of[1], (D, FF), D ** -0.5, 0.0625, ((1, 256),))
    up_weight = scatter_about(key_of[2], (D, FF), D ** -0.5, 0.0625, ((1, 256),))
    hessian_slab = scatter_about(key_of[3], (FF, SLAB), 0.2, 1.2, ((0, 32), (1, 8)), jnp.float32)
    weight_error = heavy_noise(key_of[4], (ROWS, FF), 0.03, 0.18, ((1, 32),), (1, 0, 32, 2.75), jnp.float32)
    slab_offset = jax.random.randint(key_of[5], (1,), 0, FF - SLAB + 1).astype(jnp.int32)
    token_count = jax.random.randint(key_of[6], (1,), TOK, 2 * TOK).astype(jnp.int32)
    return {"tokens": tokens, "gate_weight": gate_weight, "up_weight": up_weight, "hessian_slab": hessian_slab, "weight_error": weight_error, "slab_offset": slab_offset, "token_count": token_count}


def reference(tokens, gate_weight, up_weight, hessian_slab, weight_error, slab_offset, token_count):
    gate_pre = jnp.dot(tokens, gate_weight, preferred_element_type=jnp.float32)
    up_pre = jnp.dot(tokens, up_weight, preferred_element_type=jnp.float32)
    hidden = (jax.nn.silu(gate_pre) * up_pre).astype(jnp.bfloat16)
    first_col = slab_offset[0].astype(jnp.int32)
    window = lax.dynamic_slice_in_dim(hidden, first_col, SLAB, 1)
    gram = lax.dot_general(hidden, window, (((0,), (0,)), ((), ())), preferred_element_type=jnp.float32)
    new_slab = hessian_slab + gram / token_count[0].astype(jnp.float32)
    gradient = jnp.dot(weight_error, new_slab, precision=lax.Precision.HIGHEST, preferred_element_type=jnp.float32)
    return new_slab, gradient
```

```python
import jax
import jax.numpy as jnp
from jax import lax
from jax.experimental import pallas as pl
from jax.experimental.pallas import tpu as pltpu
from jax.sharding import Mesh
from jax.sharding import PartitionSpec as P

GR_GC = ("gr_0", "gr_1", "gr_2", "gc")
CAL_GR = ("cal", "gr_0", "gr_1", "gr_2")
CAL_GR_GC = ("cal", "gr_0", "gr_1", "gr_2", "gc")


F32 = jnp.float32
BF16 = jnp.bfloat16


def plane_index(x, y, c):
    return (((x & 1) * 2 + (x >> 1)) * 4 + y) * 2 + c


def plane_permute(array, on_x_of_core, k):
    pairs = []
    for x in range(4):
        for y in range(4):
            for c in range(2):
                to = (x ^ k, y) if c == on_x_of_core else (x, y ^ k)
                pairs.append((plane_index(x, y, c), plane_index(*to, c)))
    return lax.ppermute(array, CAL_GR, pairs)


def core_swap(array):
    return lax.ppermute(array, "gr_2", [(0, 1), (1, 0)])


def exchange(array, axes):
    return lax.all_to_all(array, axes, split_axis=0, concat_axis=0, tiled=True)


def spread(array, axes, n):
    return exchange(jnp.broadcast_to(array[None], (n, *array.shape)), axes)


VMEM = pl.BlockSpec(memory_space=pltpu.VMEM)
SMEM = pl.BlockSpec(memory_space=pltpu.SMEM)
NT = (((1,), (1,)), ((), ()))


def product_call(pos, buffers, places, own_w, far_w, before=None):
    where = [(m, g, r0) for m, g, _, r0 in places]
    steps = [b for _, _, b, _ in places]

    def kernel(pos_ref, *refs):
        toks, rest = refs[: len(buffers)], refs[len(buffers) :]
        products_body(where, [toks[b] for b in steps], before is not None, pos_ref, rest)

    shape = jax.ShapeDtypeStruct((512, own_w.shape[1]), F32)
    inputs = [pos, *buffers, own_w, far_w, *(before or ())]
    return pl.pallas_call(
        kernel,
        out_shape=(shape, shape),
        in_specs=[SMEM] + [VMEM] * (len(inputs) - 1),
        out_specs=(VMEM, VMEM),
        cost_estimate=pl.CostEstimate(
            flops=2 * 128 * len(places) * own_w.shape[2] * 2 * own_w.shape[1],
            bytes_accessed=8 << 20,
            transcendentals=0,
        ),
        name="products",
    )(*inputs)


def products_body(where, tokens, add, pos_ref, refs):
    own_w, far_w = refs[:2]
    if add:
        own_in, far_in, own_p, far_p = refs[2:]
        own_p[...] = own_in[...]
        far_p[...] = far_in[...]
    else:
        own_p, far_p = refs[2:]
        own_p[...] = jnp.zeros_like(own_p)
        far_p[...] = jnp.zeros_like(far_p)
    xl, xh, y, c = pos_ref[0], pos_ref[1], pos_ref[2], pos_ref[3]
    for (m, g, r0), t_ref in zip(where, tokens):
        t = t_ref[r0 : r0 + 128, :]
        f = xl ^ jnp.where(c == 0, g, m & 1)
        for w_ref, p_ref in ((own_w, own_p), (far_w, far_p)):
            out = lax.dot_general(t, w_ref[f], NT, preferred_element_type=F32)
            for j in range(2):
                block = jnp.where(
                    c == 0,
                    (xh ^ j) * 4 + (y ^ m),
                    (xh ^ (m >> 1)) * 4 + (y ^ (g + 2 * j)),
                )
                rows = pl.ds(pl.multiple_of(block * 64, 64), 64)
                p_ref[rows, :] += out[j * 64 : (j + 1) * 64]


def activate(own_ref, far_ref, h_ref, ht_ref):
    both = own_ref[...] + far_ref[...]
    n = both.shape[1] // 2
    gate, up = both[:, :n], both[:, n:]
    hidden = gate / (1.0 + jnp.exp(-gate)) * up
    h_ref[...] = hidden.astype(BF16)
    ht_ref[...] = hidden.T.astype(BF16)


def activate_call(own_p, far_p):
    tok, n = own_p.shape[0], own_p.shape[1] // 2
    return pl.pallas_call(
        activate,
        out_shape=(jax.ShapeDtypeStruct((tok, n), BF16), jax.ShapeDtypeStruct((n, tok), BF16)),
        in_specs=[VMEM] * 2,
        out_specs=(VMEM, VMEM),
        name="activate",
    )(own_p, far_p)


def assemble(shift_ref, y_ref, out_ref, line_ref):
    zs, ps, rows, n = y_ref.shape
    for p in range(ps):
        for z in range(zs):
            line_ref[:, pl.ds((p * zs + z) * n, n)] = y_ref[z, p].astype(F32)
    width = out_ref.shape[1]
    d = shift_ref[0]
    base = pl.multiple_of((d // 128) * 128, 128)
    near = line_ref[:, pl.ds(base, width + 128)]
    turned = pltpu.roll(near, width + 128 - (d - base), 1)
    out_ref[...] = turned[:, :width].astype(BF16)


def assemble_call(pieces, shift, width):
    zs, ps, rows, n = pieces.shape
    return pl.pallas_call(
        assemble,
        out_shape=jax.ShapeDtypeStruct((rows, width), BF16),
        in_specs=[SMEM, VMEM],
        out_specs=VMEM,
        scratch_shapes=[pltpu.VMEM((rows, zs * ps * n), F32)],
        name="assemble",
    )(shift, pieces)


def on_device(tokens, gate_weight, up_weight, hessian_slab, weight_error, slab_offset, token_count):
    xl, xh, y, c, z = (lax.axis_index(a) for a in CAL_GR_GC)
    pos = jnp.stack([xl, xh, y, c]).astype(jnp.int32)
    count = token_count[0].astype(F32)
    n = gate_weight.shape[1]
    width = hessian_slab.shape[1]
    quarter = tokens.shape[1] // 2

    parts = tokens.reshape(tokens.shape[0], 2, quarter)
    mine = lax.dynamic_index_in_dim(parts, c, 1, keepdims=False)
    theirs = core_swap(lax.dynamic_index_in_dim(parts, 1 - c, 1, keepdims=False))
    piece = jnp.concatenate([jnp.where(c == 0, mine, theirs), jnp.where(c == 0, theirs, mine)], 0)
    b0 = spread(piece, "gc", 8).reshape(64, quarter)

    def rows_of(core):
        both = [
            lax.dynamic_index_in_dim(w.T.reshape(n, 2, 2, quarter), core, 2, keepdims=False)
            for w in (gate_weight, up_weight)
        ]
        return jnp.concatenate(both, 0).swapaxes(0, 1)

    own_w = rows_of(c)
    far_w = core_swap(rows_of(1 - c))

    b1 = plane_permute(b0, 0, 1)
    b3 = plane_permute(b0, 0, 3)
    b2a = plane_permute(b1[:32], 0, 3)
    b2b = plane_permute(b3[32:], 0, 1)
    s0 = jnp.concatenate([b0, b2a, b2b, b1, b3], 0)
    s1 = plane_permute(s0, 1, 1)
    s3 = plane_permute(s0, 1, 3)
    s2a = plane_permute(s1[:128], 1, 3)
    s2b = plane_permute(s3[128:], 1, 1)
    first = product_call(
        pos,
        (s0, s1, s3),
        [(m, g, i, g * 128) for i, m in enumerate((0, 1, 3)) for g in range(2)],
        own_w,
        far_w,
    )
    own_p, far_p = product_call(pos, (s2a, s2b), [(2, 0, 0, 0), (2, 1, 1, 0)], own_w, far_w, first)
    hidden, hidden_t = activate_call(own_p, core_swap(far_p))

    chunks = exchange(hidden.reshape(32, 16, n), CAL_GR)
    panel_width = 8 * n
    starts = slab_offset[0] + jnp.arange(8, dtype=jnp.int32) * width
    panels = jnp.minimum(starts // panel_width, 29)
    wanted = jnp.stack([lax.dynamic_slice_in_dim(chunks, panels[k], 3, 0) for k in range(8)])
    pieces = exchange(wanted, "gc")
    start = slab_offset[0] + z * width
    shift = start - jnp.minimum(start // panel_width, 29) * panel_width
    chunk = assemble_call(pieces, shift.reshape(1).astype(jnp.int32), width)
    window = spread(chunk, CAL_GR, 32).reshape(512, width)

    panel_t = spread(hidden_t, "gc", 8).reshape(panel_width, 512)
    gram = jnp.dot(panel_t, window, preferred_element_type=F32)
    new_slab = hessian_slab + gram / count
    part = jnp.dot(weight_error, new_slab, precision=lax.Precision.HIGHEST, preferred_element_type=F32)
    arrived = exchange(part.reshape(32, 16, width).astype(BF16), CAL_GR)
    gradient = jnp.sum(arrived.astype(F32), axis=0)
    return (new_slab, gradient)


def solution(mesh):
    split = Mesh(
        mesh.devices.reshape(mesh.shape["cal"], 2, 4, 2, mesh.shape["gc"]),
        ("cal", "gr_0", "gr_1", "gr_2", "gc"),
    )
    return jax.shard_map(
        on_device,
        mesh=split,
        in_specs=(
            P(GR_GC, "cal"),
            P(None, CAL_GR_GC),
            P(None, CAL_GR_GC),
            P(CAL_GR, "gc"),
            P(None, CAL_GR),
            P(),
            P(),
        ),
        out_specs=(P(CAL_GR, "gc"), P(CAL_GR, "gc")),
        check_vma=False,
    )
```

```python
import jax
import jax.numpy as jnp
from jax import lax
from jax.experimental import pallas as pl
from jax.experimental.pallas import tpu as pltpu
from jax.sharding import Mesh
from jax.sharding import PartitionSpec as P

GR_GC = ("gr_0", "gr_1", "gr_2", "gc")
PLANE = ("cal", "gr_0", "gr_1")
CAL_GR = ("cal", "gr_0", "gr_1", "gr_2")
CAL_GR_GC = ("cal", "gr_0", "gr_1", "gr_2", "gc")


F32 = jnp.float32
BF16 = jnp.bfloat16
NT = (((1,), (1,)), ((), ()))
VMEM = pl.BlockSpec(memory_space=pltpu.VMEM)
SMEM = pl.BlockSpec(memory_space=pltpu.SMEM)


def plane_index(x, y, c):
    return (((x & 1) * 2 + (x >> 1)) * 4 + y) * 2 + c


def plane_permute(array, on_x_of_core, k):
    pairs = []
    for x in range(4):
        for y in range(4):
            for c in range(2):
                to = (x ^ k, y) if c == on_x_of_core else (x, y ^ k)
                pairs.append((plane_index(x, y, c), plane_index(*to, c)))
    return lax.ppermute(array, CAL_GR, pairs)


def core_swap(array):
    return lax.ppermute(array, "gr_2", [(0, 1), (1, 0)])


def shift_z(array, d):
    return lax.ppermute(array, "gc", [(i, (i + d) % 8) for i in range(8)])


def exchange(array, axes):
    return lax.all_to_all(array, axes, split_axis=0, concat_axis=0, tiled=True)


def spread(array, axes, n):
    return exchange(jnp.broadcast_to(array[None], (n, *array.shape)), axes)


def split_bf16(a):
    high = a.astype(BF16)
    return high, (a - high.astype(F32)).astype(BF16)


DEPTH = 1024


def weight_rows(refs, pad):
    gate, up = refs
    return [gate, pad, up, pad]


def product_kernel(rows_of_group, n_tok, finish, pos_ref, *refs):
    toks = refs[:n_tok]
    g0, g1, u0, u1, far_ref, own_p, far_p = refs[n_tok : n_tok + 7]
    w_ref = refs[n_tok + 7]
    k = pl.program_id(0)
    xl, c = pos_ref[0], pos_ref[3]

    @pl.when(k == 0)
    def _():
        own_p[...] = jnp.zeros_like(own_p)
        far_p[...] = jnp.zeros_like(far_p)

    pad = jnp.zeros((16, g0.shape[1]), BF16)
    halves = []
    for f, (g, u) in enumerate(((g0, u0), (g1, u1))):
        parts = [g[...], pad, u[...], pad, far_ref[2 * f], pad, far_ref[2 * f + 1], pad]
        halves.append(jnp.concatenate(parts, 0))
    same = jnp.where(xl == 0, halves[0], halves[1])
    other = jnp.where(xl == 0, halves[1], halves[0])
    w_ref[0] = same
    w_ref[1] = other
    for (odd, g), rows in rows_of_group.items():
        t = jnp.concatenate([toks[i][r0 : r0 + 128, :] for i, r0, _ in rows], 0)
        f = jnp.where(c == 0, g, odd)
        out = lax.dot_general(t, w_ref[f], NT, preferred_element_type=F32)
        for a, (_, _, m) in enumerate(rows):
            for j in range(2):
                block = finish(pos_ref, c, m, g, j)
                at = pl.ds(pl.multiple_of(block * 64, 64), 64)
                part = out[a * 128 + j * 64 : a * 128 + (j + 1) * 64]
                own_p[at, :] += part[:, :256]
                far_p[at, :] += part[:, 256:]


def block_of(pos_ref, c, m, g, j):
    xh, y = pos_ref[1], pos_ref[2]
    return jnp.where(c == 0, (xh ^ j) * 4 + (y ^ m), (xh ^ (m >> 1)) * 4 + (y ^ (g + 2 * j)))


def late_block(pos_ref, c, m, g, j):
    return jnp.where(c == 0, j, g + 2 * j)


def product_call(pos, tokens, rows_of_group, finish, blocks, gate_t, up_t, far_w):
    n, features = gate_t.shape
    depth = far_w.shape[2]
    steps = depth // DEPTH

    def kernel(pos_ref, *refs):
        product_kernel(rows_of_group, len(tokens), finish, pos_ref, *refs)

    def columns(f):
        return pl.BlockSpec((n, DEPTH), lambda k, pos: (0, (f * 2 + pos[3]) * steps + k))

    out = jax.ShapeDtypeStruct((blocks * 64, 256), F32)
    whole = pl.BlockSpec((blocks * 64, 256), lambda k, pos: (0, 0))
    rows = sum(len(r) for r in rows_of_group.values()) * 128
    return pl.pallas_call(
        kernel,
        grid_spec=pltpu.PrefetchScalarGridSpec(
            num_scalar_prefetch=1,
            grid=(steps,),
            in_specs=[pl.BlockSpec((t.shape[0], DEPTH), lambda k, pos: (0, k)) for t in tokens]
            + [columns(0), columns(1), columns(0), columns(1)]
            + [pl.BlockSpec((4, n, DEPTH), lambda k, pos: (0, 0, k))],
            out_specs=(whole, whole),
            scratch_shapes=[pltpu.VMEM((2, 512, DEPTH), BF16)],
        ),
        out_shape=(out, out),
        cost_estimate=pl.CostEstimate(
            flops=2 * rows * depth * 512, bytes_accessed=8 << 20, transcendentals=0
        ),
        name="products",
    )(pos, *tokens, gate_t, gate_t, up_t, up_t, far_w)


def activate(pos_ref, own_ref, far_ref, own_late, far_late, high_ref, low_ref, out_ref, ht_ref, sum_ref):
    c = pos_ref[3]
    xh, y = pos_ref[1], pos_ref[2]
    sum_ref[...] = own_ref[...] + far_ref[...]
    for late, core in ((own_late, c), (far_late, 1 - c)):
        for q in range(4):
            block = jnp.where(core == 0, (xh ^ (q & 1)) * 4 + (y ^ 2 ^ (q & 2)), (xh ^ 1) * 4 + (y ^ q))
            at = pl.ds(pl.multiple_of(block * 64, 64), 64)
            sum_ref[at, :] += late[q * 64 : (q + 1) * 64, :]
    both = sum_ref[...]
    gate, up = both[:, :128], both[:, 128:]
    hidden = gate / (1.0 + jnp.exp(-gate)) * up
    low = hidden.astype(BF16)
    for q in range(32):
        chunk = (q & 1) * 16 + (q >> 1)
        out_ref[q, :, :128] = low[chunk * 16 : (chunk + 1) * 16, :]
    n = ht_ref.shape[0]
    for half in range(2):
        at = pl.ds(pl.multiple_of((half ^ c) * 256, 256), 256)
        ht_ref[:, at] = hidden[half * 256 : (half + 1) * 256, :].T[:n].astype(BF16)
    part = lax.dot_general(high_ref[...], low, NT, preferred_element_type=F32)
    part += lax.dot_general(low_ref[...], low, NT, preferred_element_type=F32)
    part = part.astype(BF16)
    for q in range(32):
        out_ref[q, :, 128:] = part[q * 16 : (q + 1) * 16, :]


def activate_call(pos, own_p, far_p, own_late, far_late, error, n):
    return pl.pallas_call(
        activate,
        out_shape=(
            jax.ShapeDtypeStruct((32, 16, 128 + 512), BF16),
            jax.ShapeDtypeStruct((n, 512), BF16),
        ),
        in_specs=[SMEM] + [VMEM] * 6,
        out_specs=(VMEM, VMEM),
        scratch_shapes=[pltpu.VMEM((512, 256), F32)],
        name="activate",
    )(pos, own_p, far_p, own_late, far_late, *error)


def choose(first_ref, arrived_ref, out_ref):
    total = jnp.sum(arrived_ref[:, :, 128:].astype(F32), axis=0).astype(BF16)
    for k in range(8):
        for p in range(3):
            out_ref[k, :, p * 128 : (p + 1) * 128] = arrived_ref[first_ref[k] + p, :, :128]
        out_ref[k, :, 384:] = total


def choose_call(first, arrived):
    return pl.pallas_call(
        choose,
        out_shape=jax.ShapeDtypeStruct((8, 16, 3 * 128 + 512), BF16),
        in_specs=[SMEM, VMEM],
        out_specs=VMEM,
        name="choose",
    )(first, arrived)


def assemble(n, shift_ref, y_ref, chunk_ref, total_ref, line_ref):
    for p in range(3):
        for z in range(8):
            line_ref[:, pl.ds((p * 8 + z) * n, n)] = y_ref[z, :, p * 128 : p * 128 + n].astype(F32)
    width = chunk_ref.shape[1]
    d, c = shift_ref[0], shift_ref[1]
    base = pl.multiple_of((d // 128) * 128, 128)
    near = line_ref[:, pl.ds(base, width + 128)]
    turned = pltpu.roll(near, width + 128 - (d - base), 1)
    chunk_ref[...] = turned[:, :width].astype(BF16)
    high, low = split_bf16(jnp.sum(y_ref[:, :, 384:].astype(F32), axis=0))
    for half in range(2):
        at = pl.ds(pl.multiple_of((half ^ c) * 256, 256), 256)
        total_ref[:16, at] = high[:, half * 256 : (half + 1) * 256]
        total_ref[16:, at] = low[:, half * 256 : (half + 1) * 256]


def assemble_call(pieces, shift, width, n):
    def kernel(*refs):
        assemble(n, *refs)

    return pl.pallas_call(
        kernel,
        out_shape=(
            jax.ShapeDtypeStruct((16, width), BF16),
            jax.ShapeDtypeStruct((32, 512), BF16),
        ),
        in_specs=[SMEM, VMEM],
        out_specs=(VMEM, VMEM),
        scratch_shapes=[pltpu.VMEM((16, 24 * n), F32)],
        name="assemble",
    )(shift, pieces)


def slab_kernel(pos_ref, count_ref, *refs):
    pieces = refs[:9]
    near, far, total_ref, wh_ref, slab_ref, new_ref, grad_ref, panel_ref = refs[9:]
    z = pos_ref[4]
    n = pieces[0].shape[0]

    @pl.when(pl.program_id(0) == 0)
    def _():
        for piece, d, r0 in zip(pieces, (0, -1, 1, -2, 2, -3, 3, -4, 4), (0,) * 8 + (64,)):
            at = pl.multiple_of(((z + d + 8) % 8) * n + r0, 16)
            panel_ref[pl.ds(at, piece.shape[0]), :] = piece[...]

    count = count_ref[0].astype(F32)
    gram = jnp.dot(panel_ref[:, :256], near[...], preferred_element_type=F32)
    gram += jnp.dot(panel_ref[:, 256:], far[...], preferred_element_type=F32)
    new_ref[...] = slab_ref[...] + gram / count
    added = jnp.dot(total_ref[:, :256], near[...], preferred_element_type=F32)
    added += jnp.dot(total_ref[:, 256:], far[...], preferred_element_type=F32)
    grad_ref[...] = wh_ref[...] + (added[:16] + added[16:]) / count


def slab_call(pos, count, pieces, near, far, total, wh, slab):
    rows, width = slab.shape
    step = 256

    def fixed(a):
        return pl.BlockSpec(a.shape, lambda k, *_: (0,) * a.ndim)

    def columns(r):
        return pl.BlockSpec((r, step), lambda k, *_: (0, k))

    return pl.pallas_call(
        slab_kernel,
        grid_spec=pltpu.PrefetchScalarGridSpec(
            num_scalar_prefetch=2,
            grid=(width // step,),
            in_specs=[fixed(p) for p in pieces]
            + [columns(256), columns(256), fixed(total), columns(16), columns(rows)],
            out_specs=(columns(rows), columns(16)),
            scratch_shapes=[pltpu.VMEM((rows, 512), BF16)],
        ),
        out_shape=(
            jax.ShapeDtypeStruct((rows, width), F32),
            jax.ShapeDtypeStruct((16, width), F32),
        ),
        name="slab",
    )(pos, count, *pieces, near, far, total, wh, slab)


def on_device(tokens, gate_weight, up_weight, hessian_slab, weight_error, slab_offset, token_count):
    xl, xh, y, c, z = (lax.axis_index(a) for a in CAL_GR_GC)
    pos = jnp.stack([xl, xh, y, c, z]).astype(jnp.int32)
    n = gate_weight.shape[1]
    width = hessian_slab.shape[1]
    quarter = tokens.shape[1] // 2

    mine = lax.dynamic_slice_in_dim(tokens, c * quarter, quarter, 1)
    theirs = core_swap(lax.dynamic_slice_in_dim(tokens, (1 - c) * quarter, quarter, 1))
    piece = jnp.concatenate([jnp.where(c == 0, mine, theirs), jnp.where(c == 0, theirs, mine)], 0)
    b0 = spread(piece, "gc", 8).reshape(64, quarter)

    gate_t, up_t = gate_weight.T, up_weight.T
    far_w = core_swap(
        jnp.stack(
            [
                lax.dynamic_slice_in_dim(w, (2 * f + 1 - c) * quarter, quarter, 1)
                for f in range(2)
                for w in (gate_t, up_t)
            ]
        )
    )

    error = jnp.pad(lax.dynamic_slice_in_dim(weight_error, z * n, n, 1), ((0, 0), (0, 128 - n)))
    wh = jnp.dot(weight_error, hessian_slab, precision=lax.Precision.HIGH, preferred_element_type=F32)
    b0, wh, high, low = lax.optimization_barrier((b0, wh.astype(BF16), *split_bf16(error)))
    wh = exchange(wh.reshape(32, 16, width), CAL_GR)

    b1 = plane_permute(b0, 0, 1)
    b3 = plane_permute(b0, 0, 3)
    b2a = plane_permute(b1[:32], 0, 3)
    b2b = plane_permute(b3[32:], 0, 1)
    s0 = jnp.concatenate([b0, b2a, b2b, b1, b3], 0)
    s0, wh = lax.optimization_barrier((s0, wh))
    wh = jnp.sum(wh.astype(F32), axis=0)
    s1 = plane_permute(s0, 1, 1)
    s3 = plane_permute(s0, 1, 3)
    s2a = plane_permute(s1[:128], 1, 3)
    s2b = plane_permute(s3[128:], 1, 1)
    early = {
        (0, 0): [(0, 0, 0)],
        (0, 1): [(0, 128, 0)],
        (1, 0): [(1, 0, 1), (2, 0, 3)],
        (1, 1): [(1, 128, 1), (2, 128, 3)],
    }
    late = {(0, 0): [(0, 0, 2)], (0, 1): [(1, 0, 2)]}
    own_p, far_p = product_call(pos, (s0, s1, s3), early, block_of, 8, gate_t, up_t, far_w)
    own_q, far_q = product_call(pos, (s2a, s2b), late, late_block, 4, gate_t, up_t, far_w)
    sent, hidden_t = activate_call(
        pos, own_p, core_swap(far_p), own_q, core_swap(far_q), (high, low), n
    )

    f1, g1 = shift_z(hidden_t, 1), shift_z(hidden_t, -1)
    f2, g2 = shift_z(f1, 1), shift_z(g1, -1)
    arrived = exchange(sent, CAL_GR)
    arrived, f2, g2 = lax.optimization_barrier((arrived, f2, g2))
    f3, g3 = shift_z(f2, 1), shift_z(g2, -1)
    f4, g4 = shift_z(f3[:64], 1), shift_z(g3[64:], -1)
    panel_width = 8 * n
    starts = slab_offset[0] + jnp.arange(8, dtype=jnp.int32) * width
    pieces = exchange(choose_call(jnp.minimum(starts // panel_width, 29), arrived), "gc")
    pieces, f3, g3, f4, g4 = lax.optimization_barrier((pieces, f3, g3, f4, g4))
    start = slab_offset[0] + z * width
    shift = start - jnp.minimum(start // panel_width, 29) * panel_width
    chunk, total = assemble_call(pieces, jnp.stack([shift, c]).astype(jnp.int32), width, n)
    near = spread(chunk, PLANE, 16).reshape(256, width)
    far = core_swap(near)
    return slab_call(
        pos, token_count, (hidden_t, f1, g1, f2, g2, f3, g3, f4, g4), near, far, total, wh, hessian_slab
    )


def solution(mesh):
    split = Mesh(
        mesh.devices.reshape(mesh.shape["cal"], 2, 4, 2, mesh.shape["gc"]),
        ("cal", "gr_0", "gr_1", "gr_2", "gc"),
    )
    return jax.shard_map(
        on_device,
        mesh=split,
        in_specs=(
            P(GR_GC, "cal"),
            P(None, CAL_GR_GC),
            P(None, CAL_GR_GC),
            P(CAL_GR, "gc"),
            P(None, CAL_GR),
            P(),
            P(),
        ),
        out_specs=(P(CAL_GR, "gc"), P(CAL_GR, "gc")),
        check_vma=False,
    )
```

```python
import jax
import jax.numpy as jnp
from jax import lax
from jax.experimental import pallas as pl
from jax.experimental.pallas import tpu as pltpu
from jax.sharding import Mesh
from jax.sharding import PartitionSpec as P

GR_GC = ("gr_0", "gr_1", "gr_2", "gc")
PLANE = ("cal", "gr_0", "gr_1")
CAL_GR = ("cal", "gr_0", "gr_1", "gr_2")
CAL_GR_GC = ("cal", "gr_0", "gr_1", "gr_2", "gc")


F32 = jnp.float32
BF16 = jnp.bfloat16
NT = (((1,), (1,)), ((), ()))
VMEM = pl.BlockSpec(memory_space=pltpu.VMEM)
SMEM = pl.BlockSpec(memory_space=pltpu.SMEM)


def plane_index(x, y, c):
    return (((x & 1) * 2 + (x >> 1)) * 4 + y) * 2 + c


def plane_permute(array, on_x_of_core, k):
    pairs = []
    for x in range(4):
        for y in range(4):
            for c in range(2):
                to = (x ^ k, y) if c == on_x_of_core else (x, y ^ k)
                pairs.append((plane_index(x, y, c), plane_index(*to, c)))
    return lax.ppermute(array, CAL_GR, pairs)


def core_swap(array):
    return lax.ppermute(array, "gr_2", [(0, 1), (1, 0)])


def shift_z(array, d):
    return lax.ppermute(array, "gc", [(i, (i + d) % 8) for i in range(8)])


def exchange(array, axes):
    return lax.all_to_all(array, axes, split_axis=0, concat_axis=0, tiled=True)


def split_bf16(a):
    high = a.astype(BF16)
    return high, (a - high.astype(F32)).astype(BF16)


DEPTH = 1024


def weights_kernel(pos_ref, gate, up, far, out_ref):
    n = gate.shape[0]
    for i, part in enumerate((gate[...], up[...], far[0, 0], far[0, 1])):
        out_ref[0, i * 128 : i * 128 + n, :] = part
        out_ref[0, i * 128 + n : (i + 1) * 128, :] = jnp.zeros((128 - n, part.shape[1]), BF16)


def weights_call(pos, gate_t, up_t, far_w):
    n, depth = far_w.shape[2:]
    columns = pl.BlockSpec((n, depth), lambda f, pos: (0, (f ^ pos[0]) * 2 + pos[3]))
    return pl.pallas_call(
        weights_kernel,
        grid_spec=pltpu.PrefetchScalarGridSpec(
            num_scalar_prefetch=1,
            grid=(2,),
            in_specs=[columns, columns, pl.BlockSpec((1, 2, n, depth), lambda f, pos: (f ^ pos[0], 0, 0, 0))],
            out_specs=pl.BlockSpec((1, 512, depth), lambda f, pos: (f, 0, 0)),
        ),
        out_shape=jax.ShapeDtypeStruct((2, 512, depth), BF16),
        name="weights",
    )(pos, gate_t, up_t, far_w)


def product_kernel(rows_of_group, n_tok, finish, pos_ref, *refs):
    toks = refs[:n_tok]
    w_ref, own_p, far_p = refs[n_tok:]
    c = pos_ref[3]

    @pl.when(pl.program_id(0) == 0)
    def _():
        own_p[...] = jnp.zeros_like(own_p)
        far_p[...] = jnp.zeros_like(far_p)

    for (odd, g), rows in rows_of_group.items():
        t = jnp.concatenate([toks[i][...] for i, _ in rows], 0)
        f = jnp.where(c == 0, g, odd)
        out = lax.dot_general(t, w_ref[f], NT, preferred_element_type=F32)
        for a, (_, m) in enumerate(rows):
            for j in range(2):
                block = finish(pos_ref, c, m, g, j)
                at = pl.ds(pl.multiple_of(block * 64, 64), 64)
                part = out[a * 128 + j * 64 : a * 128 + (j + 1) * 64]
                own_p[at, :] += part[:, :256]
                far_p[at, :] += part[:, 256:]


def block_of(pos_ref, c, m, g, j):
    xh, y = pos_ref[1], pos_ref[2]
    return jnp.where(c == 0, (xh ^ j) * 4 + (y ^ m), (xh ^ (m >> 1)) * 4 + (y ^ (g + 2 * j)))


def late_block(pos_ref, c, m, g, j):
    return jnp.where(c == 0, j, g + 2 * j)


def product_call(pos, tokens, rows_of_group, finish, blocks, weights):
    depth = weights.shape[2]

    def kernel(pos_ref, *refs):
        product_kernel(rows_of_group, len(tokens), finish, pos_ref, *refs)

    out = jax.ShapeDtypeStruct((blocks * 64, 256), F32)
    whole = pl.BlockSpec((blocks * 64, 256), lambda k, pos: (0, 0))
    rows = 128 * len(tokens)
    return pl.pallas_call(
        kernel,
        grid_spec=pltpu.PrefetchScalarGridSpec(
            num_scalar_prefetch=1,
            grid=(depth // DEPTH,),
            in_specs=[pl.BlockSpec((128, DEPTH), lambda k, pos: (0, k)) for _ in tokens]
            + [pl.BlockSpec((2, 512, DEPTH), lambda k, pos: (0, 0, k))],
            out_specs=(whole, whole),
        ),
        out_shape=(out, out),
        cost_estimate=pl.CostEstimate(
            flops=2 * rows * depth * 512, bytes_accessed=8 << 20, transcendentals=0
        ),
        name="products",
    )(pos, *tokens, weights)


def activate(pos_ref, own_ref, far_ref, own_late, far_late, high_ref, low_ref, wh_ref, out_ref, ht_ref, sum_ref):
    c = pos_ref[3]
    xh, y = pos_ref[1], pos_ref[2]
    sum_ref[...] = own_ref[...] + far_ref[...]
    for late, core in ((own_late, c), (far_late, 1 - c)):
        for q in range(4):
            block = jnp.where(core == 0, (xh ^ (q & 1)) * 4 + (y ^ 2 ^ (q & 2)), (xh ^ 1) * 4 + (y ^ q))
            at = pl.ds(pl.multiple_of(block * 64, 64), 64)
            sum_ref[at, :] += late[q * 64 : (q + 1) * 64, :]
    both = sum_ref[...]
    gate, up = both[:, :128], both[:, 128:]
    hidden = gate / (1.0 + jnp.exp(-gate)) * up
    low = hidden.astype(BF16)
    for q in range(32):
        chunk = (q & 1) * 16 + (q >> 1)
        out_ref[q, :, :128] = low[chunk * 16 : (chunk + 1) * 16, :]
    n = ht_ref.shape[0]
    for half in range(2):
        at = pl.ds(pl.multiple_of((half ^ c) * 256, 256), 256)
        ht_ref[:, at] = hidden[half * 256 : (half + 1) * 256, :].T[:n].astype(BF16)
    part = lax.dot_general(high_ref[...], low, NT, preferred_element_type=F32)
    part += lax.dot_general(low_ref[...], low, NT, preferred_element_type=F32)
    part = part.astype(BF16)
    for q in range(32):
        out_ref[q, :, 128:640] = part[q * 16 : (q + 1) * 16, :]
        out_ref[q, :, 640:] = wh_ref[q * 16 : (q + 1) * 16, :]


def activate_call(pos, own_p, far_p, own_late, far_late, error, wh, n):
    return pl.pallas_call(
        activate,
        out_shape=(
            jax.ShapeDtypeStruct((32, 16, 640 + wh.shape[1]), BF16),
            jax.ShapeDtypeStruct((n, 512), BF16),
        ),
        in_specs=[SMEM] + [VMEM] * 7,
        out_specs=(VMEM, VMEM),
        scratch_shapes=[pltpu.VMEM((512, 256), F32)],
        name="activate",
    )(pos, own_p, far_p, own_late, far_late, *error, wh)


def choose(first_ref, arrived_ref, out_ref, wh_ref):
    total = jnp.sum(arrived_ref[:, :, 128:640].astype(F32), axis=0).astype(BF16)
    half = wh_ref.shape[1] // 2
    for core in range(2):
        sums = arrived_ref[core, :, 640:].astype(F32)
        for k in range(1, 16):
            sums += arrived_ref[2 * k + core, :, 640:].astype(F32)
        wh_ref[:, core * half : (core + 1) * half] = sums
    for k in range(8):
        for p in range(3):
            out_ref[k, :, p * 128 : (p + 1) * 128] = arrived_ref[first_ref[k] + p, :, :128]
        out_ref[k, :, 384:] = total


def choose_call(first, arrived):
    return pl.pallas_call(
        choose,
        out_shape=(
            jax.ShapeDtypeStruct((8, 16, 3 * 128 + 512), BF16),
            jax.ShapeDtypeStruct((16, 2 * (arrived.shape[2] - 640)), F32),
        ),
        in_specs=[SMEM, VMEM],
        out_specs=(VMEM, VMEM),
        name="choose",
    )(first, arrived)


def assemble(n, shift_ref, y_ref, chunk_ref, total_ref, line_ref):
    for p in range(3):
        for z in range(8):
            line_ref[:, pl.ds((p * 8 + z) * n, n)] = y_ref[z, :, p * 128 : p * 128 + n].astype(F32)
    width = chunk_ref.shape[2]
    d, c = shift_ref[0], shift_ref[1]
    base = pl.multiple_of((d // 128) * 128, 128)
    near = line_ref[:, pl.ds(base, width + 128)]
    turned = pltpu.roll(near, width + 128 - (d - base), 1)
    chunk = turned[:, :width].astype(BF16)
    for k in range(chunk_ref.shape[0]):
        chunk_ref[k] = chunk
    high, low = split_bf16(jnp.sum(y_ref[:, :, 384:].astype(F32), axis=0))
    for half in range(2):
        at = pl.ds(pl.multiple_of((half ^ c) * 256, 256), 256)
        total_ref[:16, at] = high[:, half * 256 : (half + 1) * 256]
        total_ref[16:, at] = low[:, half * 256 : (half + 1) * 256]


def assemble_call(pieces, shift, width, n):
    def kernel(*refs):
        assemble(n, *refs)

    return pl.pallas_call(
        kernel,
        out_shape=(
            jax.ShapeDtypeStruct((16, 16, width), BF16),
            jax.ShapeDtypeStruct((32, 512), BF16),
        ),
        in_specs=[SMEM, VMEM],
        out_specs=(VMEM, VMEM),
        scratch_shapes=[pltpu.VMEM((16, 24 * n), F32)],
        name="assemble",
    )(shift, pieces)


def slab_kernel(pos_ref, count_ref, *refs):
    pieces = refs[:9]
    near, far, total_ref, wh_ref, slab_ref, new_ref, grad_ref, panel_ref = refs[9:]
    z = pos_ref[4]
    n = pieces[0].shape[0]

    @pl.when(pl.program_id(0) == 0)
    def _():
        for piece, d, r0 in zip(pieces, (0, -1, 1, -2, 2, -3, 3, -4, 4), (0,) * 8 + (64,)):
            at = pl.multiple_of(((z + d + 8) % 8) * n + r0, 16)
            panel_ref[pl.ds(at, piece.shape[0]), :] = piece[...]

    scale = 1.0 / jnp.full((1, 1), count_ref[0].astype(F32), F32)
    gram = jnp.dot(panel_ref[:, :256], near[...], preferred_element_type=F32)
    gram += jnp.dot(panel_ref[:, 256:], far[...], preferred_element_type=F32)
    new_ref[...] = slab_ref[...] + gram * scale
    added = jnp.dot(total_ref[:, :256], near[...], preferred_element_type=F32)
    added += jnp.dot(total_ref[:, 256:], far[...], preferred_element_type=F32)
    grad_ref[...] = wh_ref[...] + (added[:16] + added[16:]) * scale


def slab_call(pos, count, pieces, near, far, total, wh, slab):
    rows, width = slab.shape
    step = 256

    def fixed(a):
        return pl.BlockSpec(a.shape, lambda k, *_: (0,) * a.ndim)

    def columns(r):
        return pl.BlockSpec((r, step), lambda k, *_: (0, k))

    return pl.pallas_call(
        slab_kernel,
        grid_spec=pltpu.PrefetchScalarGridSpec(
            num_scalar_prefetch=2,
            grid=(width // step,),
            in_specs=[fixed(p) for p in pieces]
            + [columns(256), columns(256), fixed(total), columns(16), columns(rows)],
            out_specs=(columns(rows), columns(16)),
            scratch_shapes=[pltpu.VMEM((rows, 512), BF16)],
        ),
        out_shape=(
            jax.ShapeDtypeStruct((rows, width), F32),
            jax.ShapeDtypeStruct((16, width), F32),
        ),
        name="slab",
    )(pos, count, *pieces, near, far, total, wh, slab)


def on_device(tokens, gate_weight, up_weight, hessian_slab, weight_error, slab_offset, token_count):
    xl, xh, y, c, z = (lax.axis_index(a) for a in CAL_GR_GC)
    pos = jnp.stack([xl, xh, y, c, z]).astype(jnp.int32)
    n = gate_weight.shape[1]
    width = hessian_slab.shape[1]
    quarter = tokens.shape[1] // 2

    mine = lax.dynamic_slice_in_dim(tokens, c * quarter, quarter, 1)
    theirs = core_swap(lax.dynamic_slice_in_dim(tokens, (1 - c) * quarter, quarter, 1))
    piece = jnp.concatenate([jnp.where(c == 0, mine, theirs), jnp.where(c == 0, theirs, mine)], 0)
    copies = jnp.broadcast_to(piece[None], (8, *piece.shape))
    copies, gate_weight, up_weight, weight_error = lax.optimization_barrier(
        (copies, gate_weight, up_weight, weight_error)
    )
    b0 = exchange(copies, "gc").reshape(64, quarter)
    gate_t, up_t = gate_weight.T, up_weight.T
    far_w = core_swap(
        jnp.stack(
            [
                lax.dynamic_slice_in_dim(w, (2 * f + 1 - c) * quarter, quarter, 1)
                for f in range(2)
                for w in (gate_t, up_t)
            ]
        )
    )

    error = jnp.pad(lax.dynamic_slice_in_dim(weight_error, z * n, n, 1), ((0, 0), (0, 128 - n)))
    wh = jnp.dot(weight_error, hessian_slab, precision=lax.Precision.HIGH, preferred_element_type=F32)
    b0, wh, far_w, high, low = lax.optimization_barrier((b0, wh, far_w, *split_bf16(error)))

    b1 = plane_permute(b0, 0, 1)
    b3 = plane_permute(b0, 0, 3)
    half = width // 2
    wh_far = core_swap(lax.dynamic_slice_in_dim(wh, (1 - c) * half, half, 1))
    wh = (lax.dynamic_slice_in_dim(wh, c * half, half, 1) + wh_far).astype(BF16)
    weights = weights_call(pos, gate_t, up_t, far_w.reshape(2, 2, n, quarter))
    b1, b3, weights = lax.optimization_barrier((b1, b3, weights))
    b2a = plane_permute(b1[:32], 0, 3)
    b2b = plane_permute(b3[32:], 0, 1)
    b2a, b2b, wh = lax.optimization_barrier((b2a, b2b, wh))
    sb = jnp.concatenate([b1, b3], 0)
    s3b = plane_permute(sb, 1, 3)
    s1b = plane_permute(sb, 1, 1)
    sa = jnp.concatenate([b0, b2a, b2b], 0)
    s1a = plane_permute(sa, 1, 1)
    s3a = plane_permute(sa, 1, 3)
    s2b = plane_permute(s3b, 1, 1)
    s2a = plane_permute(s1a, 1, 3)
    early = {(0, 0): [(0, 0)], (0, 1): [(1, 0)], (1, 0): [(2, 1), (3, 3)], (1, 1): [(4, 1), (5, 3)]}
    late = {(0, 0): [(0, 2)], (0, 1): [(1, 2)]}
    own_p, far_p = product_call(pos, (sa, sb, s1a, s3a, s1b, s3b), early, block_of, 8, weights)
    own_q, far_q = product_call(pos, (s2a, s2b), late, late_block, 4, weights)
    sent, hidden_t = activate_call(
        pos, own_p, core_swap(far_p), own_q, core_swap(far_q), (high, low), wh, n
    )

    f1, g1 = shift_z(hidden_t, 1), shift_z(hidden_t, -1)
    f2, g2 = shift_z(f1, 1), shift_z(g1, -1)
    f3, g3 = shift_z(f2, 1), shift_z(g2, -1)
    arrived = exchange(sent, CAL_GR)
    arrived, f3, g3 = lax.optimization_barrier((arrived, f3, g3))
    f4, g4 = shift_z(f3[:64], 1), shift_z(g3[64:], -1)
    panel_width = 8 * n
    starts = slab_offset[0] + jnp.arange(8, dtype=jnp.int32) * width
    wanted, wh = choose_call(jnp.minimum(starts // panel_width, 29), arrived)
    pieces = exchange(wanted, "gc")
    pieces, f4, g4 = lax.optimization_barrier((pieces, f4, g4))
    start = slab_offset[0] + z * width
    shift = start - jnp.minimum(start // panel_width, 29) * panel_width
    chunk, total = assemble_call(pieces, jnp.stack([shift, c]).astype(jnp.int32), width, n)
    near = exchange(chunk, PLANE).reshape(256, width)
    far = core_swap(near)
    return slab_call(
        pos, token_count, (hidden_t, f1, g1, f2, g2, f3, g3, f4, g4), near, far, total, wh, hessian_slab
    )


def solution(mesh):
    split = Mesh(
        mesh.devices.reshape(mesh.shape["cal"], 2, 4, 2, mesh.shape["gc"]),
        ("cal", "gr_0", "gr_1", "gr_2", "gc"),
    )

    return jax.shard_map(
        on_device,
        mesh=split,
        in_specs=(
            P(GR_GC, "cal"),
            P(None, CAL_GR_GC),
            P(None, CAL_GR_GC),
            P(CAL_GR, "gc"),
            P(None, CAL_GR),
            P(),
            P(),
        ),
        out_specs=(P(CAL_GR, "gc"), P(CAL_GR, "gc")),
        check_vma=False,
    )
```

```python
import jax
import jax.numpy as jnp
from jax import lax
from jax.experimental import pallas as pl
from jax.experimental.pallas import tpu as pltpu
from jax.sharding import Mesh
from jax.sharding import PartitionSpec as P

GR_GC = ("gr_0", "gr_1", "gr_2", "gc")
PLANE = ("cal", "gr_0", "gr_1")
CAL_GR = ("cal", "gr_0", "gr_1", "gr_2")
CAL_GR_GC = ("cal", "gr_0", "gr_1", "gr_2", "gc")


F32 = jnp.float32
BF16 = jnp.bfloat16
NT = (((1,), (1,)), ((), ()))
VMEM = pl.BlockSpec(memory_space=pltpu.VMEM)
SMEM = pl.BlockSpec(memory_space=pltpu.SMEM)


def plane_index(x, y, c):
    return (((x & 1) * 2 + (x >> 1)) * 4 + y) * 2 + c


def plane_permute(array, on_x_of_core, k):
    pairs = []
    for x in range(4):
        for y in range(4):
            for c in range(2):
                to = (x ^ k, y) if c == on_x_of_core else (x, y ^ k)
                pairs.append((plane_index(x, y, c), plane_index(*to, c)))
    return lax.ppermute(array, CAL_GR, pairs)


def core_swap(array):
    return lax.ppermute(array, "gr_2", [(0, 1), (1, 0)])


def shift_z(array, d):
    return lax.ppermute(array, "gc", [(i, (i + d) % 8) for i in range(8)])


def exchange(array, axes):
    return lax.all_to_all(array, axes, split_axis=0, concat_axis=0, tiled=True)


def split_bf16(a):
    high = a.astype(BF16)
    return high, (a - high.astype(F32)).astype(BF16)


GROUPS = ((0, 0), (0, 1), (1, 0), (1, 1), (3, 0), (3, 1), (2, 0), (2, 1))


def weights_kernel(pos_ref, gate, up, far, out_ref):
    n = gate.shape[0]
    for i, part in enumerate((gate[...], up[...], far[0, 0], far[0, 1])):
        out_ref[0, i * 128 : i * 128 + n, :] = part
        out_ref[0, i * 128 + n : (i + 1) * 128, :] = jnp.zeros((128 - n, part.shape[1]), BF16)


def weights_call(pos, gate_t, up_t, far_w):
    n, depth = far_w.shape[2:]
    columns = pl.BlockSpec((n, depth), lambda f, pos: (0, (f ^ pos[0]) * 2 + pos[3]))
    return pl.pallas_call(
        weights_kernel,
        grid_spec=pltpu.PrefetchScalarGridSpec(
            num_scalar_prefetch=1,
            grid=(2,),
            in_specs=[columns, columns, pl.BlockSpec((1, 2, n, depth), lambda f, pos: (f ^ pos[0], 0, 0, 0))],
            out_specs=pl.BlockSpec((1, 512, depth), lambda f, pos: (f, 0, 0)),
        ),
        out_shape=jax.ShapeDtypeStruct((2, 512, depth), BF16),
        name="weights",
    )(pos, gate_t, up_t, far_w)


def products(tokens, weights, f):
    w = weights[f] if isinstance(f, int) else lax.dynamic_index_in_dim(weights, f, 0, keepdims=False)
    return [lax.dot_general(tokens, half, NT, preferred_element_type=F32) for half in (w[:256], w[256:])]


def activate(pos_ref, *refs):
    own, far = refs[:8], refs[8:10]
    high_ref, low_ref, wh_ref, out_ref, ht_ref, sum_ref = refs[10:]
    c = pos_ref[3]
    xh, y = pos_ref[1], pos_ref[2]
    sum_ref[...] = jnp.zeros_like(sum_ref)
    for i, (m, g) in enumerate(GROUPS):
        theirs = far[0][i * 128 : (i + 1) * 128, :] if i < 6 else far[1][(i - 6) * 128 : (i - 5) * 128, :]
        for core, part in ((c, own[i][...]), (1 - c, theirs)):
            for j in range(2):
                block = jnp.where(
                    core == 0,
                    (xh ^ j) * 4 + (y ^ m),
                    (xh ^ (m >> 1)) * 4 + (y ^ (g + 2 * j)),
                )
                at = pl.ds(pl.multiple_of(block * 64, 64), 64)
                sum_ref[at, :] += part[j * 64 : (j + 1) * 64]
    both = sum_ref[...]
    gate, up = both[:, :128], both[:, 128:]
    hidden = gate / (1.0 + jnp.exp(-gate)) * up
    low = hidden.astype(BF16)
    for q in range(32):
        chunk = (q & 1) * 16 + (q >> 1)
        out_ref[q, :, :128] = low[chunk * 16 : (chunk + 1) * 16, :]
    n = ht_ref.shape[0]
    for half in range(2):
        at = pl.ds(pl.multiple_of((half ^ c) * 256, 256), 256)
        ht_ref[:, at] = hidden[half * 256 : (half + 1) * 256, :].T[:n].astype(BF16)
    part = lax.dot_general(high_ref[...], low, NT, preferred_element_type=F32)
    part += lax.dot_general(low_ref[...], low, NT, preferred_element_type=F32)
    part = part.astype(BF16)
    for q in range(32):
        out_ref[q, :, 128:640] = part[q * 16 : (q + 1) * 16, :]
        out_ref[q, :, 640:] = wh_ref[q * 16 : (q + 1) * 16, :]


def activate_call(pos, own, far, error, wh, n):
    return pl.pallas_call(
        activate,
        out_shape=(
            jax.ShapeDtypeStruct((32, 16, 640 + wh.shape[1]), BF16),
            jax.ShapeDtypeStruct((n, 512), BF16),
        ),
        in_specs=[SMEM] + [VMEM] * 13,
        out_specs=(VMEM, VMEM),
        scratch_shapes=[pltpu.VMEM((512, 256), F32)],
        name="activate",
    )(pos, *own, *far, *error, wh)


def choose(first_ref, arrived_ref, out_ref):
    total = jnp.sum(arrived_ref[:, :, 128:].astype(F32), axis=0).astype(BF16)
    for k in range(8):
        for p in range(3):
            out_ref[k, :, p * 128 : (p + 1) * 128] = arrived_ref[first_ref[k] + p, :, :128]
        out_ref[k, :, 384:] = total


def choose_call(first, arrived):
    return pl.pallas_call(
        choose,
        grid_spec=pltpu.PrefetchScalarGridSpec(
            num_scalar_prefetch=1,
            grid=(1,),
            in_specs=[pl.BlockSpec((32, 16, 640), lambda i, first: (0, 0, 0))],
            out_specs=pl.BlockSpec((8, 16, 896), lambda i, first: (0, 0, 0)),
        ),
        out_shape=jax.ShapeDtypeStruct((8, 16, 896), BF16),
        name="choose",
    )(first, arrived)


def assemble(n, shift_ref, y_ref, chunk_ref, total_ref, line_ref):
    for p in range(3):
        for z in range(8):
            line_ref[:, pl.ds((p * 8 + z) * n, n)] = y_ref[z, :, p * 128 : p * 128 + n].astype(F32)
    width = chunk_ref.shape[2]
    d, c = shift_ref[0], shift_ref[1]
    base = pl.multiple_of((d // 128) * 128, 128)
    near = line_ref[:, pl.ds(base, width + 128)]
    turned = pltpu.roll(near, width + 128 - (d - base), 1)
    chunk = turned[:, :width].astype(BF16)
    for k in range(chunk_ref.shape[0]):
        chunk_ref[k] = chunk
    high, low = split_bf16(jnp.sum(y_ref[:, :, 384:].astype(F32), axis=0))
    for half in range(2):
        at = pl.ds(pl.multiple_of((half ^ c) * 256, 256), 256)
        total_ref[:16, at] = high[:, half * 256 : (half + 1) * 256]
        total_ref[16:, at] = low[:, half * 256 : (half + 1) * 256]


def assemble_call(pieces, shift, width, n):
    def kernel(*refs):
        assemble(n, *refs)

    return pl.pallas_call(
        kernel,
        out_shape=(
            jax.ShapeDtypeStruct((16, 16, width), BF16),
            jax.ShapeDtypeStruct((32, 512), BF16),
        ),
        in_specs=[SMEM, VMEM],
        out_specs=(VMEM, VMEM),
        scratch_shapes=[pltpu.VMEM((16, 24 * n), F32)],
        name="assemble",
    )(shift, pieces)


def panel_kernel(pos_ref, *refs):
    panel_ref = refs[-1]
    z = pos_ref[4]
    n = refs[0].shape[0]
    for piece, d, r0 in zip(refs[:9], (0, -1, 1, -2, 2, -3, 3, -4, 4), (0,) * 8 + (64,)):
        at = pl.multiple_of(((z + d + 8) % 8) * n + r0, 16)
        panel_ref[pl.ds(at, piece.shape[0]), :] = piece[...]


def panel_call(pos, pieces):
    rows = 8 * pieces[0].shape[0]
    return pl.pallas_call(
        panel_kernel,
        out_shape=jax.ShapeDtypeStruct((rows, 512), BF16),
        in_specs=[SMEM] + [VMEM] * len(pieces),
        out_specs=VMEM,
        name="panel",
    )(pos, *pieces)


def on_device(tokens, gate_weight, up_weight, hessian_slab, weight_error, slab_offset, token_count):
    xl, xh, y, c, z = (lax.axis_index(a) for a in CAL_GR_GC)
    pos = jnp.stack([xl, xh, y, c, z]).astype(jnp.int32)
    n = gate_weight.shape[1]
    width = hessian_slab.shape[1]
    quarter = tokens.shape[1] // 2

    mine = lax.dynamic_slice_in_dim(tokens, c * quarter, quarter, 1)
    theirs = core_swap(lax.dynamic_slice_in_dim(tokens, (1 - c) * quarter, quarter, 1))
    piece = jnp.concatenate([jnp.where(c == 0, mine, theirs), jnp.where(c == 0, theirs, mine)], 0)
    copies = jnp.broadcast_to(piece[None], (8, *piece.shape))
    copies, gate_weight, up_weight, weight_error = lax.optimization_barrier(
        (copies, gate_weight, up_weight, weight_error)
    )
    b0 = exchange(copies, "gc").reshape(64, quarter)
    gate_t, up_t = gate_weight.T, up_weight.T
    far_w = core_swap(
        jnp.stack(
            [
                lax.dynamic_slice_in_dim(w, (2 * f + 1 - c) * quarter, quarter, 1)
                for f in range(2)
                for w in (gate_t, up_t)
            ]
        )
    )

    error = jnp.pad(lax.dynamic_slice_in_dim(weight_error, z * n, n, 1), ((0, 0), (0, 128 - n)))
    half = width // 2
    wh_own, wh_sent = (
        jnp.dot(
            weight_error,
            lax.dynamic_slice_in_dim(hessian_slab, core * half, half, 1),
            precision=lax.Precision.HIGH,
            preferred_element_type=F32,
        )
        for core in (c, 1 - c)
    )
    b0, wh_own, wh_sent, far_w, high, low = lax.optimization_barrier(
        (b0, wh_own, wh_sent, far_w, *split_bf16(error))
    )

    b1 = plane_permute(b0, 0, 1)
    b3 = plane_permute(b0, 0, 3)
    wh_far = core_swap(wh_sent)
    wh = (wh_own + wh_far).astype(BF16)
    weights = weights_call(pos, gate_t, up_t, far_w.reshape(2, 2, n, quarter))
    b1, b3, weights = lax.optimization_barrier((b1, b3, weights))
    b2a = plane_permute(b1[:32], 0, 3)
    b2b = plane_permute(b3[32:], 0, 1)
    b2a, b2b, wh = lax.optimization_barrier((b2a, b2b, wh))
    sb = jnp.concatenate([b1, b3], 0)
    s3b = plane_permute(sb, 1, 3)
    s1b = plane_permute(sb, 1, 1)
    sa = jnp.concatenate([b0, b2a, b2b], 0)
    s1a = plane_permute(sa, 1, 1)
    s3a = plane_permute(sa, 1, 3)
    s2b = plane_permute(s3b, 1, 1)
    s2a = plane_permute(s1a, 1, 3)
    own, far = [], []
    for buffer, f in zip((sa, sb, s1a, s1b, s3a, s3b, s2a, s2b), (0, 1 - c, c, 1, c, 1, 0, 1 - c)):
        mine, theirs = products(buffer, weights, f)
        own.append(mine)
        far.append(theirs)
    far = [core_swap(jnp.concatenate(part, 0)) for part in (far[:6], far[6:])]
    sent, hidden_t = activate_call(pos, own, far, (high, low), wh, n)

    f1, g1 = shift_z(hidden_t, 1), shift_z(hidden_t, -1)
    f2, g2 = shift_z(f1, 1), shift_z(g1, -1)
    arrived = exchange(sent, CAL_GR)
    arrived, f2, g2 = lax.optimization_barrier((arrived, f2, g2))
    f3, g3 = shift_z(f2, 1), shift_z(g2, -1)
    panel_width = 8 * n
    starts = slab_offset[0] + jnp.arange(8, dtype=jnp.int32) * width
    pieces = exchange(choose_call(jnp.minimum(starts // panel_width, 29), arrived), "gc")
    sums = jnp.sum(arrived[:, :, 640:].reshape(16, 2, 16, half).astype(F32), axis=0)
    wh = jnp.concatenate([sums[0], sums[1]], 1)
    pieces, f3, g3, wh = lax.optimization_barrier((pieces, f3, g3, wh))
    f4, g4 = shift_z(f3[:64], 1), shift_z(g3[64:], -1)
    start = slab_offset[0] + z * width
    shift = start - jnp.minimum(start // panel_width, 29) * panel_width
    chunk, total = assemble_call(pieces, jnp.stack([shift, c]).astype(jnp.int32), width, n)
    near = exchange(chunk, PLANE).reshape(256, width)
    panel_t = panel_call(pos, (hidden_t, f1, g1, f2, g2, f3, g3, f4, g4))
    near, panel_t = lax.optimization_barrier((near, panel_t))
    window = jnp.concatenate([near, core_swap(near)], 0)
    scale = 1.0 / token_count[0].astype(F32)
    gram = jnp.dot(panel_t, window, preferred_element_type=F32)
    added = jnp.dot(total, window, preferred_element_type=F32)
    return (hessian_slab + gram * scale, wh + (added[:16] + added[16:]) * scale)


def solution(mesh):
    split = Mesh(
        mesh.devices.reshape(mesh.shape["cal"], 2, 4, 2, mesh.shape["gc"]),
        ("cal", "gr_0", "gr_1", "gr_2", "gc"),
    )

    return jax.shard_map(
        on_device,
        mesh=split,
        in_specs=(
            P(GR_GC, "cal"),
            P(None, CAL_GR_GC),
            P(None, CAL_GR_GC),
            P(CAL_GR, "gc"),
            P(None, CAL_GR),
            P(),
            P(),
        ),
        out_specs=(P(CAL_GR, "gc"), P(CAL_GR, "gc")),
        check_vma=False,
    )
```

```python
import jax
import jax.numpy as jnp
from jax import lax
from jax.experimental import pallas as pl
from jax.experimental.pallas import tpu as pltpu
from jax.sharding import Mesh
from jax.sharding import PartitionSpec as P

GR_GC = ("gr_0", "gr_1", "gr_2", "gc")
PLANE = ("cal", "gr_0", "gr_1")
CAL_GR = ("cal", "gr_0", "gr_1", "gr_2")
CAL_GR_GC = ("cal", "gr_0", "gr_1", "gr_2", "gc")


F32 = jnp.float32
BF16 = jnp.bfloat16
NT = (((1,), (1,)), ((), ()))
VMEM = pl.BlockSpec(memory_space=pltpu.VMEM)
SMEM = pl.BlockSpec(memory_space=pltpu.SMEM)


def plane_index(x, y, c):
    return (((x & 1) * 2 + (x >> 1)) * 4 + y) * 2 + c


def plane_permute(array, on_x_of_core, k):
    pairs = []
    for x in range(4):
        for y in range(4):
            for c in range(2):
                to = (x ^ k, y) if c == on_x_of_core else (x, y ^ k)
                pairs.append((plane_index(x, y, c), plane_index(*to, c)))
    return lax.ppermute(array, CAL_GR, pairs)


def core_swap(array):
    return lax.ppermute(array, "gr_2", [(0, 1), (1, 0)])


def shift_z(array, d):
    return lax.ppermute(array, "gc", [(i, (i + d) % 8) for i in range(8)])


def exchange(array, axes):
    return lax.all_to_all(array, axes, split_axis=0, concat_axis=0, tiled=True)


def split_bf16(a):
    high = a.astype(BF16)
    return high, (a - high.astype(F32)).astype(BF16)


GROUPS = ((0, 0), (0, 1), (1, 0), (1, 1), (3, 0), (3, 1), (2, 0), (2, 1))


def weights_kernel(pos_ref, gate, up, far, out_ref):
    n = gate.shape[0]
    for i, part in enumerate((gate[...], up[...], far[0, 0], far[0, 1])):
        out_ref[0, i * 128 : i * 128 + n, :] = part
        out_ref[0, i * 128 + n : (i + 1) * 128, :] = jnp.zeros((128 - n, part.shape[1]), BF16)


def weights_call(pos, gate_t, up_t, far_w):
    n, depth = far_w.shape[2:]
    columns = pl.BlockSpec((n, depth), lambda f, pos: (0, (f ^ pos[0]) * 2 + pos[3]))
    return pl.pallas_call(
        weights_kernel,
        grid_spec=pltpu.PrefetchScalarGridSpec(
            num_scalar_prefetch=1,
            grid=(2,),
            in_specs=[columns, columns, pl.BlockSpec((1, 2, n, depth), lambda f, pos: (f ^ pos[0], 0, 0, 0))],
            out_specs=pl.BlockSpec((1, 512, depth), lambda f, pos: (f, 0, 0)),
        ),
        out_shape=jax.ShapeDtypeStruct((2, 512, depth), BF16),
        name="weights",
    )(pos, gate_t, up_t, far_w)


def products(tokens, weights, f):
    w = weights[f] if isinstance(f, int) else lax.dynamic_index_in_dim(weights, f, 0, keepdims=False)
    return [lax.dot_general(tokens, half, NT, preferred_element_type=F32) for half in (w[:256], w[256:])]


def activate(pos_ref, *refs):
    own, far = refs[:8], refs[8:10]
    high_ref, low_ref, wh_ref, out_ref, ht_ref, sum_ref = refs[10:]
    c = pos_ref[3]
    xh, y = pos_ref[1], pos_ref[2]
    sum_ref[...] = jnp.zeros_like(sum_ref)
    for i, (m, g) in enumerate(GROUPS):
        theirs = far[0][i * 128 : (i + 1) * 128, :] if i < 6 else far[1][(i - 6) * 128 : (i - 5) * 128, :]
        for core, part in ((c, own[i][...]), (1 - c, theirs)):
            for j in range(2):
                block = jnp.where(
                    core == 0,
                    (xh ^ j) * 4 + (y ^ m),
                    (xh ^ (m >> 1)) * 4 + (y ^ (g + 2 * j)),
                )
                at = pl.ds(pl.multiple_of(block * 64, 64), 64)
                sum_ref[at, :] += part[j * 64 : (j + 1) * 64]
    both = sum_ref[...]
    gate, up = both[:, :128], both[:, 128:]
    hidden = gate / (1.0 + jnp.exp(-gate)) * up
    low = hidden.astype(BF16)
    for q in range(32):
        chunk = (q & 1) * 16 + (q >> 1)
        out_ref[q, :, :128] = low[chunk * 16 : (chunk + 1) * 16, :]
    n = ht_ref.shape[0]
    for half in range(2):
        at = pl.ds(pl.multiple_of((half ^ c) * 256, 256), 256)
        ht_ref[:, at] = hidden[half * 256 : (half + 1) * 256, :].T[:n].astype(BF16)
    part = lax.dot_general(high_ref[...], low, NT, preferred_element_type=F32)
    part += lax.dot_general(low_ref[...], low, NT, preferred_element_type=F32)
    part = part.astype(BF16)
    for q in range(32):
        out_ref[q, :, 128:640] = part[q * 16 : (q + 1) * 16, :]
        out_ref[q, :, 640:] = wh_ref[q * 16 : (q + 1) * 16, :]


def activate_call(pos, own, far, error, wh, n):
    return pl.pallas_call(
        activate,
        out_shape=(
            jax.ShapeDtypeStruct((32, 16, 640 + wh.shape[1]), BF16),
            jax.ShapeDtypeStruct((n, 512), BF16),
        ),
        in_specs=[SMEM] + [VMEM] * 13,
        out_specs=(VMEM, VMEM),
        scratch_shapes=[pltpu.VMEM((512, 256), F32)],
        name="activate",
    )(pos, *own, *far, *error, wh)


def choose(first_ref, arrived_ref, out_ref):
    total = jnp.sum(arrived_ref[:, :, 128:].astype(F32), axis=0).astype(BF16)
    for k in range(8):
        for p in range(3):
            out_ref[k, :, p * 128 : (p + 1) * 128] = arrived_ref[first_ref[k] + p, :, :128]
        out_ref[k, :, 384:] = total


def choose_call(first, arrived):
    return pl.pallas_call(
        choose,
        grid_spec=pltpu.PrefetchScalarGridSpec(
            num_scalar_prefetch=1,
            grid=(1,),
            in_specs=[pl.BlockSpec((32, 16, 640), lambda i, first: (0, 0, 0))],
            out_specs=pl.BlockSpec((8, 16, 896), lambda i, first: (0, 0, 0)),
        ),
        out_shape=jax.ShapeDtypeStruct((8, 16, 896), BF16),
        name="choose",
    )(first, arrived)


def assemble(n, shift_ref, y_ref, chunk_ref, total_ref, line_ref):
    for p in range(3):
        for z in range(8):
            line_ref[:, pl.ds((p * 8 + z) * n, n)] = y_ref[z, :, p * 128 : p * 128 + n].astype(F32)
    width = chunk_ref.shape[2]
    d, c = shift_ref[0], shift_ref[1]
    base = pl.multiple_of((d // 128) * 128, 128)
    near = line_ref[:, pl.ds(base, width + 128)]
    turned = pltpu.roll(near, width + 128 - (d - base), 1)
    chunk = turned[:, :width].astype(BF16)
    for k in range(chunk_ref.shape[0]):
        chunk_ref[k] = chunk
    high, low = split_bf16(jnp.sum(y_ref[:, :, 384:].astype(F32), axis=0))
    for half in range(2):
        at = pl.ds(pl.multiple_of((half ^ c) * 256, 256), 256)
        total_ref[:16, at] = high[:, half * 256 : (half + 1) * 256]
        total_ref[16:, at] = low[:, half * 256 : (half + 1) * 256]


def assemble_call(pieces, shift, width, n):
    def kernel(*refs):
        assemble(n, *refs)

    return pl.pallas_call(
        kernel,
        out_shape=(
            jax.ShapeDtypeStruct((16, 16, width), BF16),
            jax.ShapeDtypeStruct((32, 512), BF16),
        ),
        in_specs=[SMEM, VMEM],
        out_specs=(VMEM, VMEM),
        scratch_shapes=[pltpu.VMEM((16, 24 * n), F32)],
        name="assemble",
    )(shift, pieces)


def slab_kernel(pos_ref, count_ref, *refs):
    pieces = refs[:9]
    near, far, total_ref, wh_ref, slab_ref, new_ref, grad_ref, panel_ref = refs[9:]
    z = pos_ref[4]
    n = pieces[0].shape[0]

    @pl.when(pl.program_id(0) == 0)
    def _():
        for piece, d, r0 in zip(pieces, (0, -1, 1, -2, 2, -3, 3, -4, 4), (0,) * 8 + (64,)):
            at = pl.multiple_of(((z + d + 8) % 8) * n + r0, 16)
            panel_ref[pl.ds(at, piece.shape[0]), :] = piece[...]

    scale = 1.0 / jnp.full((1, 1), count_ref[0].astype(F32), F32)
    gram = jnp.dot(panel_ref[:, :256], near[...], preferred_element_type=F32)
    gram += jnp.dot(panel_ref[:, 256:], far[...], preferred_element_type=F32)
    new_ref[...] = slab_ref[...] + gram * scale
    added = jnp.dot(total_ref[:, :256], near[...], preferred_element_type=F32)
    added += jnp.dot(total_ref[:, 256:], far[...], preferred_element_type=F32)
    grad_ref[...] = wh_ref[...] + (added[:16] + added[16:]) * scale


def slab_call(pos, count, pieces, near, far, total, wh, slab):
    rows, width = slab.shape
    step = 512

    def fixed(a):
        return pl.BlockSpec(a.shape, lambda k, *_: (0,) * a.ndim)

    def columns(r):
        return pl.BlockSpec((r, step), lambda k, *_: (0, k))

    return pl.pallas_call(
        slab_kernel,
        grid_spec=pltpu.PrefetchScalarGridSpec(
            num_scalar_prefetch=2,
            grid=(width // step,),
            in_specs=[fixed(p) for p in pieces]
            + [columns(256), columns(256), fixed(total), columns(16), columns(rows)],
            out_specs=(columns(rows), columns(16)),
            scratch_shapes=[pltpu.VMEM((rows, 512), BF16)],
        ),
        out_shape=(
            jax.ShapeDtypeStruct((rows, width), F32),
            jax.ShapeDtypeStruct((16, width), F32),
        ),
        name="slab",
    )(pos, count, *pieces, near, far, total, wh, slab)


def on_device(tokens, gate_weight, up_weight, hessian_slab, weight_error, slab_offset, token_count):
    xl, xh, y, c, z = (lax.axis_index(a) for a in CAL_GR_GC)
    pos = jnp.stack([xl, xh, y, c, z]).astype(jnp.int32)
    n = gate_weight.shape[1]
    width = hessian_slab.shape[1]
    quarter = tokens.shape[1] // 2

    mine = lax.dynamic_slice_in_dim(tokens, c * quarter, quarter, 1)
    theirs = core_swap(lax.dynamic_slice_in_dim(tokens, (1 - c) * quarter, quarter, 1))
    piece = jnp.concatenate([jnp.where(c == 0, mine, theirs), jnp.where(c == 0, theirs, mine)], 0)
    copies = jnp.broadcast_to(piece[None], (8, *piece.shape))
    copies, gate_weight, up_weight, weight_error = lax.optimization_barrier(
        (copies, gate_weight, up_weight, weight_error)
    )
    b0 = exchange(copies, "gc").reshape(64, quarter)
    gate_t, up_t = gate_weight.T, up_weight.T
    far_w = core_swap(
        jnp.stack(
            [
                lax.dynamic_slice_in_dim(w, (2 * f + 1 - c) * quarter, quarter, 1)
                for f in range(2)
                for w in (gate_t, up_t)
            ]
        )
    )

    error = jnp.pad(lax.dynamic_slice_in_dim(weight_error, z * n, n, 1), ((0, 0), (0, 128 - n)))
    half = width // 2
    wh_own, wh_sent = (
        jnp.dot(
            weight_error,
            lax.dynamic_slice_in_dim(hessian_slab, core * half, half, 1),
            precision=lax.Precision.HIGH,
            preferred_element_type=F32,
        )
        for core in (c, 1 - c)
    )
    b0, wh_own, wh_sent, far_w, high, low = lax.optimization_barrier(
        (b0, wh_own, wh_sent, far_w, *split_bf16(error))
    )

    b1 = plane_permute(b0, 0, 1)
    b3 = plane_permute(b0, 0, 3)
    b2 = plane_permute(b0, 0, 2)
    weights = weights_call(pos, gate_t, up_t, far_w.reshape(2, 2, n, quarter))
    sb = jnp.concatenate([b1, b3], 0)
    s3b = plane_permute(sb, 1, 3)
    s1b = plane_permute(sb, 1, 1)
    sa = jnp.concatenate([b0, b2], 0)
    s1a = plane_permute(sa, 1, 1)
    s3a = plane_permute(sa, 1, 3)
    s2b = plane_permute(s3b, 1, 1)
    s2a = plane_permute(s1a, 1, 3)
    wh_far = core_swap(wh_sent)
    wh = (wh_own + wh_far).astype(BF16)
    own, far = [], []
    for buffer, f in zip((sa, sb, s1a, s1b, s3a, s3b, s2a, s2b), (0, 1 - c, c, 1, c, 1, 0, 1 - c)):
        mine, theirs = products(buffer, weights, f)
        own.append(mine)
        far.append(theirs)
    far = [jnp.concatenate(part, 0) for part in (far[:6], far[6:])]
    far = [core_swap(part) for part in far]
    sent, hidden_t = activate_call(pos, own, far, (high, low), wh, n)

    f1, g1 = shift_z(hidden_t, 1), shift_z(hidden_t, -1)
    f2, g2 = shift_z(f1, 1), shift_z(g1, -1)
    arrived = exchange(sent, CAL_GR)
    arrived, f2, g2 = lax.optimization_barrier((arrived, f2, g2))
    f3, g3 = shift_z(f2, 1), shift_z(g2, -1)
    panel_width = 8 * n
    starts = slab_offset[0] + jnp.arange(8, dtype=jnp.int32) * width
    wanted = choose_call(jnp.minimum(starts // panel_width, 29), arrived)
    pieces = exchange(wanted, "gc")
    sums = jnp.sum(arrived[:, :, 640:].reshape(16, 2, 16, half).astype(F32), axis=0)
    wh = jnp.concatenate([sums[0], sums[1]], 1)
    pieces, f3, g3, wh = lax.optimization_barrier((pieces, f3, g3, wh))
    f4, g4 = shift_z(f3[:64], 1), shift_z(g3[64:], -1)
    start = slab_offset[0] + z * width
    shift = start - jnp.minimum(start // panel_width, 29) * panel_width
    chunk, total = assemble_call(pieces, jnp.stack([shift, c]).astype(jnp.int32), width, n)
    near = exchange(chunk, PLANE).reshape(256, width)
    return slab_call(
        pos, token_count, (hidden_t, f1, g1, f2, g2, f3, g3, f4, g4), near, core_swap(near), total, wh, hessian_slab
    )


def solution(mesh):
    split = Mesh(
        mesh.devices.reshape(mesh.shape["cal"], 2, 4, 2, mesh.shape["gc"]),
        ("cal", "gr_0", "gr_1", "gr_2", "gc"),
    )

    return jax.shard_map(
        on_device,
        mesh=split,
        in_specs=(
            P(GR_GC, "cal"),
            P(None, CAL_GR_GC),
            P(None, CAL_GR_GC),
            P(CAL_GR, "gc"),
            P(None, CAL_GR),
            P(),
            P(),
        ),
        out_specs=(P(CAL_GR, "gc"), P(CAL_GR, "gc")),
        check_vma=False,
    )
```

```python
import jax
import jax.numpy as jnp
from jax import lax
from jax.experimental import pallas as pl
from jax.experimental.pallas import tpu as pltpu
from jax.sharding import Mesh
from jax.sharding import PartitionSpec as P

GR_GC = ("gr_0", "gr_1", "gr_2", "gc")
PLANE = ("cal", "gr_0", "gr_1")
CAL_GR = ("cal", "gr_0", "gr_1", "gr_2")
CAL_GR_GC = ("cal", "gr_0", "gr_1", "gr_2", "gc")


F32 = jnp.float32
BF16 = jnp.bfloat16
NT = (((1,), (1,)), ((), ()))
VMEM = pl.BlockSpec(memory_space=pltpu.VMEM)
SMEM = pl.BlockSpec(memory_space=pltpu.SMEM)


def plane_index(x, y, c):
    return (((x & 1) * 2 + (x >> 1)) * 4 + y) * 2 + c


def plane_permute(array, on_x_of_core, k):
    pairs = []
    for x in range(4):
        for y in range(4):
            for c in range(2):
                to = (x ^ k, y) if c == on_x_of_core else (x, y ^ k)
                pairs.append((plane_index(x, y, c), plane_index(*to, c)))
    return lax.ppermute(array, CAL_GR, pairs)


def core_swap(array):
    return lax.ppermute(array, "gr_2", [(0, 1), (1, 0)])


def shift_z(array, d):
    return lax.ppermute(array, "gc", [(i, (i + d) % 8) for i in range(8)])


def exchange(array, axes):
    return lax.all_to_all(array, axes, split_axis=0, concat_axis=0, tiled=True)


def split_bf16(a):
    high = a.astype(BF16)
    return high, (a - high.astype(F32)).astype(BF16)


GROUPS = ((0, 0), (0, 1), (1, 0), (1, 1), (3, 0), (3, 1), (2, 0), (2, 1))


def weights_kernel(pos_ref, gate, up, far, out_ref):
    n = gate.shape[0]
    for i, part in enumerate((gate[...], up[...], far[0, 0], far[0, 1])):
        out_ref[0, i * 128 : i * 128 + n, :] = part
        out_ref[0, i * 128 + n : (i + 1) * 128, :] = jnp.zeros((128 - n, part.shape[1]), BF16)


def weights_call(pos, gate_t, up_t, far_w):
    n, depth = far_w.shape[2:]
    columns = pl.BlockSpec((n, depth), lambda f, pos: (0, (f ^ pos[0]) * 2 + pos[3]))
    return pl.pallas_call(
        weights_kernel,
        grid_spec=pltpu.PrefetchScalarGridSpec(
            num_scalar_prefetch=1,
            grid=(2,),
            in_specs=[columns, columns, pl.BlockSpec((1, 2, n, depth), lambda f, pos: (f ^ pos[0], 0, 0, 0))],
            out_specs=pl.BlockSpec((1, 512, depth), lambda f, pos: (f, 0, 0)),
        ),
        out_shape=jax.ShapeDtypeStruct((2, 512, depth), BF16),
        name="weights",
    )(pos, gate_t, up_t, far_w)


def products(tokens, weights, f):
    w = weights[f] if isinstance(f, int) else lax.dynamic_index_in_dim(weights, f, 0, keepdims=False)
    return [lax.dot_general(tokens, half, NT, preferred_element_type=F32) for half in (w[:256], w[256:])]


def activate(pos_ref, *refs):
    own, far = refs[:2], refs[2:4]
    high_ref, low_ref, wh_ref, out_ref, ht_ref, sum_ref = refs[4:]
    c = pos_ref[3]
    xh, y = pos_ref[1], pos_ref[2]
    sum_ref[...] = jnp.zeros_like(sum_ref)
    for i, (m, g) in enumerate(GROUPS):
        late, at = i // 6, slice(i % 6 * 128, i % 6 * 128 + 128)
        for core, part in ((c, own[late][at, :]), (1 - c, far[late][at, :])):
            for j in range(2):
                block = jnp.where(
                    core == 0,
                    (xh ^ j) * 4 + (y ^ m),
                    (xh ^ (m >> 1)) * 4 + (y ^ (g + 2 * j)),
                )
                at = pl.ds(pl.multiple_of(block * 64, 64), 64)
                sum_ref[at, :] += part[j * 64 : (j + 1) * 64]
    both = sum_ref[...]
    gate, up = both[:, :128], both[:, 128:]
    hidden = gate / (1.0 + jnp.exp(-gate)) * up
    low = hidden.astype(BF16)
    for q in range(32):
        chunk = (q & 1) * 16 + (q >> 1)
        out_ref[q, :, :128] = low[chunk * 16 : (chunk + 1) * 16, :]
    n = ht_ref.shape[0]
    for half in range(2):
        at = pl.ds(pl.multiple_of((half ^ c) * 256, 256), 256)
        ht_ref[:, at] = hidden[half * 256 : (half + 1) * 256, :].T[:n].astype(BF16)
    part = lax.dot_general(high_ref[...], low, NT, preferred_element_type=F32)
    part += lax.dot_general(low_ref[...], low, NT, preferred_element_type=F32)
    part = part.astype(BF16)
    for q in range(32):
        out_ref[q, :, 128:640] = part[q * 16 : (q + 1) * 16, :]
        out_ref[q, :, 640:] = wh_ref[q * 16 : (q + 1) * 16, :]


def activate_call(pos, own, far, error, wh, n):
    return pl.pallas_call(
        activate,
        out_shape=(
            jax.ShapeDtypeStruct((32, 16, 640 + wh.shape[1]), BF16),
            jax.ShapeDtypeStruct((n, 512), BF16),
        ),
        in_specs=[SMEM] + [VMEM] * 7,
        out_specs=(VMEM, VMEM),
        scratch_shapes=[pltpu.VMEM((512, 256), F32)],
        name="activate",
    )(pos, *own, *far, *error, wh)


def choose(first_ref, arrived_ref, out_ref):
    total = jnp.sum(arrived_ref[:, :, 128:].astype(F32), axis=0).astype(BF16)
    for k in range(8):
        for p in range(3):
            out_ref[k, :, p * 128 : (p + 1) * 128] = arrived_ref[first_ref[k] + p, :, :128]
        out_ref[k, :, 384:] = total


def choose_call(first, arrived):
    return pl.pallas_call(
        choose,
        grid_spec=pltpu.PrefetchScalarGridSpec(
            num_scalar_prefetch=1,
            grid=(1,),
            in_specs=[pl.BlockSpec((32, 16, 640), lambda i, first: (0, 0, 0))],
            out_specs=pl.BlockSpec((8, 16, 896), lambda i, first: (0, 0, 0)),
        ),
        out_shape=jax.ShapeDtypeStruct((8, 16, 896), BF16),
        name="choose",
    )(first, arrived)


def assemble(n, shift_ref, y_ref, chunk_ref, total_ref, line_ref):
    for p in range(3):
        for z in range(8):
            line_ref[:, pl.ds((p * 8 + z) * n, n)] = y_ref[z, :, p * 128 : p * 128 + n].astype(F32)
    width = chunk_ref.shape[2]
    d, c = shift_ref[0], shift_ref[1]
    base = pl.multiple_of((d // 128) * 128, 128)
    near = line_ref[:, pl.ds(base, width + 128)]
    turned = pltpu.roll(near, width + 128 - (d - base), 1)
    chunk = turned[:, :width].astype(BF16)
    for k in range(chunk_ref.shape[0]):
        chunk_ref[k] = chunk
    high, low = split_bf16(jnp.sum(y_ref[:, :, 384:].astype(F32), axis=0))
    for half in range(2):
        at = pl.ds(pl.multiple_of((half ^ c) * 256, 256), 256)
        total_ref[:16, at] = high[:, half * 256 : (half + 1) * 256]
        total_ref[16:, at] = low[:, half * 256 : (half + 1) * 256]


def assemble_call(pieces, shift, width, n):
    def kernel(*refs):
        assemble(n, *refs)

    return pl.pallas_call(
        kernel,
        out_shape=(
            jax.ShapeDtypeStruct((16, 16, width), BF16),
            jax.ShapeDtypeStruct((32, 512), BF16),
        ),
        in_specs=[SMEM, VMEM],
        out_specs=(VMEM, VMEM),
        scratch_shapes=[pltpu.VMEM((16, 24 * n), F32)],
        name="assemble",
    )(shift, pieces)


def slab_kernel(pos_ref, count_ref, *refs):
    pieces = refs[:8]
    near, far, total_ref, wh_ref, slab_ref, new_ref, grad_ref, panel_ref = refs[8:]
    z = pos_ref[4]
    n = pieces[0].shape[0]

    @pl.when(pl.program_id(0) == 0)
    def _():
        for piece, d in zip(pieces, (0, -1, 1, -2, 2, -3, 3, 4)):
            at = pl.multiple_of(((z + d + 8) % 8) * n, 16)
            panel_ref[pl.ds(at, piece.shape[0]), :] = piece[...]

    scale = 1.0 / jnp.full((1, 1), count_ref[0].astype(F32), F32)
    gram = jnp.dot(panel_ref[:, :256], near[...], preferred_element_type=F32)
    gram += jnp.dot(panel_ref[:, 256:], far[...], preferred_element_type=F32)
    new_ref[...] = slab_ref[...] + gram * scale
    added = jnp.dot(total_ref[:, :256], near[...], preferred_element_type=F32)
    added += jnp.dot(total_ref[:, 256:], far[...], preferred_element_type=F32)
    grad_ref[...] = wh_ref[...] + (added[:16] + added[16:]) * scale


def slab_call(pos, count, pieces, near, far, total, wh, slab):
    rows, width = slab.shape
    step = 512

    def fixed(a):
        return pl.BlockSpec(a.shape, lambda k, *_: (0,) * a.ndim)

    def columns(r):
        return pl.BlockSpec((r, step), lambda k, *_: (0, k))

    return pl.pallas_call(
        slab_kernel,
        grid_spec=pltpu.PrefetchScalarGridSpec(
            num_scalar_prefetch=2,
            grid=(width // step,),
            in_specs=[fixed(p) for p in pieces]
            + [columns(256), columns(256), fixed(total), columns(16), columns(rows)],
            out_specs=(columns(rows), columns(16)),
            scratch_shapes=[pltpu.VMEM((rows, 512), BF16)],
        ),
        out_shape=(
            jax.ShapeDtypeStruct((rows, width), F32),
            jax.ShapeDtypeStruct((16, width), F32),
        ),
        name="slab",
    )(pos, count, *pieces, near, far, total, wh, slab)


def on_device(tokens, gate_weight, up_weight, hessian_slab, weight_error, slab_offset, token_count):
    xl, xh, y, c, z = (lax.axis_index(a) for a in CAL_GR_GC)
    pos = jnp.stack([xl, xh, y, c, z]).astype(jnp.int32)
    n = gate_weight.shape[1]
    width = hessian_slab.shape[1]
    quarter = tokens.shape[1] // 2

    mine = lax.dynamic_slice_in_dim(tokens, c * quarter, quarter, 1)
    theirs = core_swap(lax.dynamic_slice_in_dim(tokens, (1 - c) * quarter, quarter, 1))
    piece = jnp.concatenate([jnp.where(c == 0, mine, theirs), jnp.where(c == 0, theirs, mine)], 0)
    copies = jnp.broadcast_to(piece[None], (8, *piece.shape))
    copies, gate_weight, up_weight, weight_error = lax.optimization_barrier(
        (copies, gate_weight, up_weight, weight_error)
    )
    b0 = exchange(copies, "gc").reshape(64, quarter)
    gate_t, up_t = gate_weight.T, up_weight.T
    far_w = core_swap(
        jnp.stack(
            [
                lax.dynamic_slice_in_dim(w, (2 * f + 1 - c) * quarter, quarter, 1)
                for f in range(2)
                for w in (gate_t, up_t)
            ]
        )
    )

    error = jnp.pad(lax.dynamic_slice_in_dim(weight_error, z * n, n, 1), ((0, 0), (0, 128 - n)))
    half = width // 2
    wh_own, wh_sent = (
        jnp.dot(
            weight_error,
            lax.dynamic_slice_in_dim(hessian_slab, core * half, half, 1),
            precision=lax.Precision.HIGH,
            preferred_element_type=F32,
        )
        for core in (c, 1 - c)
    )
    b0, wh_own, wh_sent, far_w, high, low = lax.optimization_barrier(
        (b0, wh_own, wh_sent, far_w, *split_bf16(error))
    )

    b1 = plane_permute(b0, 0, 1)
    b3 = plane_permute(b0, 0, 3)
    b2a = plane_permute(b1[:32], 0, 3)
    b2b = plane_permute(b3[32:], 0, 1)
    weights = weights_call(pos, gate_t, up_t, far_w.reshape(2, 2, n, quarter))
    sb = jnp.concatenate([b1, b3], 0)
    s3b = plane_permute(sb, 1, 3)
    s1b = plane_permute(sb, 1, 1)
    sa = jnp.concatenate([b0, b2a, b2b], 0)
    s1a = plane_permute(sa, 1, 1)
    s3a = plane_permute(sa, 1, 3)
    s2b = plane_permute(s3b, 1, 1)
    s2a = plane_permute(s1a, 1, 3)
    wh_far = core_swap(wh_sent)
    wh = (wh_own + wh_far).astype(BF16)
    own, far = [], []
    for buffer, f in zip((sa, sb, s1a, s1b, s3a, s3b, s2a, s2b), (0, 1 - c, c, 1, c, 1, 0, 1 - c)):
        mine, theirs = products(buffer, weights, f)
        own.append(mine)
        far.append(theirs)
    own, far = ([jnp.concatenate(part, 0) for part in (all_of[:6], all_of[6:])] for all_of in (own, far))
    far = [core_swap(part) for part in far]
    sent, hidden_t = activate_call(pos, own, far, (high, low), wh, n)

    f1, g1 = shift_z(hidden_t, 1), shift_z(hidden_t, -1)
    f2, g2 = shift_z(f1, 1), shift_z(g1, -1)
    arrived = exchange(sent, CAL_GR)
    arrived, f2, g2 = lax.optimization_barrier((arrived, f2, g2))
    f3, g3 = shift_z(f2, 1), shift_z(g2, -1)
    panel_width = 8 * n
    starts = slab_offset[0] + jnp.arange(8, dtype=jnp.int32) * width
    wanted = choose_call(jnp.minimum(starts // panel_width, 29), arrived)
    pieces = exchange(wanted, "gc")
    sums = jnp.sum(arrived[:, :, 640:].reshape(16, 2, 16, half).astype(F32), axis=0)
    wh = jnp.concatenate([sums[0], sums[1]], 1)
    pieces, wh = lax.optimization_barrier((pieces, wh))
    f4, g4 = shift_z(f3[:64], 1), shift_z(g3[64:], -1)
    h4 = jnp.concatenate([f4, g4], 0)
    start = slab_offset[0] + z * width
    shift = start - jnp.minimum(start // panel_width, 29) * panel_width
    chunk, total = assemble_call(pieces, jnp.stack([shift, c]).astype(jnp.int32), width, n)
    near = exchange(chunk, PLANE).reshape(256, width)
    return slab_call(
        pos, token_count, (hidden_t, f1, g1, f2, g2, f3, g3, h4), near, core_swap(near), total, wh, hessian_slab
    )


def solution(mesh):
    split = Mesh(
        mesh.devices.reshape(mesh.shape["cal"], 2, 4, 2, mesh.shape["gc"]),
        ("cal", "gr_0", "gr_1", "gr_2", "gc"),
    )

    return jax.shard_map(
        on_device,
        mesh=split,
        in_specs=(
            P(GR_GC, "cal"),
            P(None, CAL_GR_GC),
            P(None, CAL_GR_GC),
            P(CAL_GR, "gc"),
            P(None, CAL_GR),
            P(),
            P(),
        ),
        out_specs=(P(CAL_GR, "gc"), P(CAL_GR, "gc")),
        check_vma=False,
    )
```

```python
import jax
import jax.numpy as jnp
from jax import lax
from jax.experimental import pallas as pl
from jax.experimental.pallas import tpu as pltpu
from jax.sharding import Mesh
from jax.sharding import PartitionSpec as P

GR_GC = ("gr_0", "gr_1", "gr_2", "gc")
PLANE = ("cal", "gr_0", "gr_1")
CAL_GR = ("cal", "gr_0", "gr_1", "gr_2")
CAL_GR_GC = ("cal", "gr_0", "gr_1", "gr_2", "gc")


F32 = jnp.float32
BF16 = jnp.bfloat16
NT = (((1,), (1,)), ((), ()))
VMEM = pl.BlockSpec(memory_space=pltpu.VMEM)
SMEM = pl.BlockSpec(memory_space=pltpu.SMEM)


def plane_index(x, y, c):
    return (((x & 1) * 2 + (x >> 1)) * 4 + y) * 2 + c


def plane_permute(array, on_x_of_core, k):
    pairs = []
    for x in range(4):
        for y in range(4):
            for c in range(2):
                to = (x ^ k, y) if c == on_x_of_core else (x, y ^ k)
                pairs.append((plane_index(x, y, c), plane_index(*to, c)))
    return lax.ppermute(array, CAL_GR, pairs)


def core_swap(array):
    return lax.ppermute(array, "gr_2", [(0, 1), (1, 0)])


def shift_z(array, d):
    return lax.ppermute(array, "gc", [(i, (i + d) % 8) for i in range(8)])


def exchange(array, axes):
    return lax.all_to_all(array, axes, split_axis=0, concat_axis=0, tiled=True)


def split_bf16(a):
    high = a.astype(BF16)
    return high, (a - high.astype(F32)).astype(BF16)


GROUPS = ((0, 0), (0, 1), (1, 0), (1, 1), (3, 0), (3, 1), (2, 0), (2, 1))


def weights_kernel(pos_ref, gate, up, far, out_ref):
    n = gate.shape[0]
    for i, part in enumerate((gate[...], up[...], far[0, 0], far[0, 1])):
        out_ref[0, i * 128 : i * 128 + n, :] = part
        out_ref[0, i * 128 + n : (i + 1) * 128, :] = jnp.zeros((128 - n, part.shape[1]), BF16)


def weights_call(pos, gate_t, up_t, far_w):
    n, depth = far_w.shape[2:]
    columns = pl.BlockSpec((n, depth), lambda f, pos: (0, (f ^ pos[0]) * 2 + pos[3]))
    return pl.pallas_call(
        weights_kernel,
        grid_spec=pltpu.PrefetchScalarGridSpec(
            num_scalar_prefetch=1,
            grid=(2,),
            in_specs=[columns, columns, pl.BlockSpec((1, 2, n, depth), lambda f, pos: (f ^ pos[0], 0, 0, 0))],
            out_specs=pl.BlockSpec((1, 512, depth), lambda f, pos: (f, 0, 0)),
        ),
        out_shape=jax.ShapeDtypeStruct((2, 512, depth), BF16),
        compiler_params=pltpu.CompilerParams(vmem_limit_bytes=12 << 20),
        name="weights",
    )(pos, gate_t, up_t, far_w)


def products(tokens, weights, f):
    w = weights[f] if isinstance(f, int) else lax.dynamic_index_in_dim(weights, f, 0, keepdims=False)
    return [lax.dot_general(tokens, half, NT, preferred_element_type=F32) for half in (w[:256], w[256:])]


def activate(pos_ref, *refs):
    own, far = refs[:8], refs[8:10]
    high_ref, low_ref, wh_ref, out_ref, ht_ref, sum_ref = refs[10:]
    c = pos_ref[3]
    xh, y = pos_ref[1], pos_ref[2]
    sum_ref[...] = jnp.zeros_like(sum_ref)
    for i, (m, g) in enumerate(GROUPS):
        theirs = far[0][i * 128 : (i + 1) * 128, :] if i < 6 else far[1][(i - 6) * 128 : (i - 5) * 128, :]
        for core, part in ((c, own[i][...]), (1 - c, theirs)):
            for j in range(2):
                block = jnp.where(
                    core == 0,
                    (xh ^ j) * 4 + (y ^ m),
                    (xh ^ (m >> 1)) * 4 + (y ^ (g + 2 * j)),
                )
                at = pl.ds(pl.multiple_of(block * 64, 64), 64)
                sum_ref[at, :] += part[j * 64 : (j + 1) * 64]
    both = sum_ref[...]
    gate, up = both[:, :128], both[:, 128:]
    hidden = gate / (1.0 + jnp.exp(-gate)) * up
    low = hidden.astype(BF16)
    for q in range(32):
        chunk = (q & 1) * 16 + (q >> 1)
        out_ref[q, :, :128] = low[chunk * 16 : (chunk + 1) * 16, :]
    n = ht_ref.shape[0]
    for half in range(2):
        at = pl.ds(pl.multiple_of((half ^ c) * 256, 256), 256)
        ht_ref[:, at] = hidden[half * 256 : (half + 1) * 256, :].T[:n].astype(BF16)
    part = lax.dot_general(high_ref[...], low, NT, preferred_element_type=F32)
    part += lax.dot_general(low_ref[...], low, NT, preferred_element_type=F32)
    part = part.astype(BF16)
    for q in range(32):
        out_ref[q, :, 128:640] = part[q * 16 : (q + 1) * 16, :]
        out_ref[q, :, 640:] = wh_ref[q * 16 : (q + 1) * 16, :]


def activate_call(pos, own, far, error, wh, n):
    return pl.pallas_call(
        activate,
        out_shape=(
            jax.ShapeDtypeStruct((32, 16, 640 + wh.shape[1]), BF16),
            jax.ShapeDtypeStruct((n, 512), BF16),
        ),
        in_specs=[SMEM] + [VMEM] * 13,
        out_specs=(VMEM, VMEM),
        scratch_shapes=[pltpu.VMEM((512, 256), F32)],
        compiler_params=pltpu.CompilerParams(vmem_limit_bytes=12 << 20),
        name="activate",
    )(pos, *own, *far, *error, wh)


def choose(first_ref, arrived_ref, out_ref):
    total = jnp.sum(arrived_ref[:, :, 128:].astype(F32), axis=0).astype(BF16)
    for k in range(8):
        for p in range(3):
            out_ref[k, :, p * 128 : (p + 1) * 128] = arrived_ref[first_ref[k] + p, :, :128]
        out_ref[k, :, 384:] = total


def choose_call(first, arrived):
    return pl.pallas_call(
        choose,
        grid_spec=pltpu.PrefetchScalarGridSpec(
            num_scalar_prefetch=1,
            grid=(1,),
            in_specs=[pl.BlockSpec((32, 16, 640), lambda i, first: (0, 0, 0))],
            out_specs=pl.BlockSpec((8, 16, 896), lambda i, first: (0, 0, 0)),
        ),
        out_shape=jax.ShapeDtypeStruct((8, 16, 896), BF16),
        compiler_params=pltpu.CompilerParams(vmem_limit_bytes=6 << 20),
        name="choose",
    )(first, arrived)


def assemble(n, shift_ref, y_ref, chunk_ref, total_ref, line_ref):
    for p in range(3):
        for z in range(8):
            line_ref[:, pl.ds((p * 8 + z) * n, n)] = y_ref[z, :, p * 128 : p * 128 + n].astype(F32)
    width = chunk_ref.shape[2]
    d, c = shift_ref[0], shift_ref[1]
    base = pl.multiple_of((d // 128) * 128, 128)
    near = line_ref[:, pl.ds(base, width + 128)]
    turned = pltpu.roll(near, width + 128 - (d - base), 1)
    chunk = turned[:, :width].astype(BF16)
    for k in range(chunk_ref.shape[0]):
        chunk_ref[k] = chunk
    high, low = split_bf16(jnp.sum(y_ref[:, :, 384:].astype(F32), axis=0))
    for half in range(2):
        at = pl.ds(pl.multiple_of((half ^ c) * 256, 256), 256)
        total_ref[:16, at] = high[:, half * 256 : (half + 1) * 256]
        total_ref[16:, at] = low[:, half * 256 : (half + 1) * 256]


def assemble_call(pieces, shift, width, n):
    def kernel(*refs):
        assemble(n, *refs)

    return pl.pallas_call(
        kernel,
        out_shape=(
            jax.ShapeDtypeStruct((16, 16, width), BF16),
            jax.ShapeDtypeStruct((32, 512), BF16),
        ),
        in_specs=[SMEM, VMEM],
        out_specs=(VMEM, VMEM),
        scratch_shapes=[pltpu.VMEM((16, 24 * n), F32)],
        compiler_params=pltpu.CompilerParams(vmem_limit_bytes=6 << 20),
        name="assemble",
    )(shift, pieces)


def slab_kernel(pos_ref, count_ref, *refs):
    pieces = refs[:8]
    near, far, total_ref, wh_ref, slab_ref, new_ref, grad_ref, panel_ref = refs[8:]
    z = pos_ref[4]
    n = pieces[0].shape[0]

    @pl.when(pl.program_id(0) == 0)
    def _():
        for piece, d in zip(pieces, (0, -1, 1, -2, 2, -3, 3, 4)):
            at = pl.multiple_of(((z + d + 8) % 8) * n, 16)
            panel_ref[pl.ds(at, piece.shape[0]), :] = piece[...]

    scale = 1.0 / jnp.full((1, 1), count_ref[0].astype(F32), F32)
    gram = jnp.dot(panel_ref[:, :256], near[...], preferred_element_type=F32)
    gram += jnp.dot(panel_ref[:, 256:], far[...], preferred_element_type=F32)
    new_ref[...] = slab_ref[...] + gram * scale
    added = jnp.dot(total_ref[:, :256], near[...], preferred_element_type=F32)
    added += jnp.dot(total_ref[:, 256:], far[...], preferred_element_type=F32)
    grad_ref[...] = wh_ref[...] + (added[:16] + added[16:]) * scale


def slab_call(pos, count, pieces, near, far, total, wh, slab):
    rows, width = slab.shape
    step = 512

    def fixed(a):
        return pl.BlockSpec(a.shape, lambda k, *_: (0,) * a.ndim)

    def columns(r):
        return pl.BlockSpec((r, step), lambda k, *_: (0, k))

    return pl.pallas_call(
        slab_kernel,
        grid_spec=pltpu.PrefetchScalarGridSpec(
            num_scalar_prefetch=2,
            grid=(width // step,),
            in_specs=[fixed(p) for p in pieces]
            + [columns(256), columns(256), fixed(total), columns(16), columns(rows)],
            out_specs=(columns(rows), columns(16)),
            scratch_shapes=[pltpu.VMEM((rows, 512), BF16)],
        ),
        out_shape=(
            jax.ShapeDtypeStruct((rows, width), F32),
            jax.ShapeDtypeStruct((16, width), F32),
        ),
        compiler_params=pltpu.CompilerParams(vmem_limit_bytes=20 << 20),
        name="slab",
    )(pos, count, *pieces, near, far, total, wh, slab)


def on_device(tokens, gate_weight, up_weight, hessian_slab, weight_error, slab_offset, token_count):
    xl, xh, y, c, z = (lax.axis_index(a) for a in CAL_GR_GC)
    pos = jnp.stack([xl, xh, y, c, z]).astype(jnp.int32)
    n = gate_weight.shape[1]
    width = hessian_slab.shape[1]
    quarter = tokens.shape[1] // 2

    mine = lax.dynamic_slice_in_dim(tokens, c * quarter, quarter, 1)
    theirs = core_swap(lax.dynamic_slice_in_dim(tokens, (1 - c) * quarter, quarter, 1))
    piece = jnp.concatenate([jnp.where(c == 0, mine, theirs), jnp.where(c == 0, theirs, mine)], 0)
    copies = jnp.broadcast_to(piece[None], (8, *piece.shape))
    copies, gate_weight, up_weight, weight_error = lax.optimization_barrier(
        (copies, gate_weight, up_weight, weight_error)
    )
    b0 = exchange(copies, "gc").reshape(64, quarter)
    gate_t, up_t = gate_weight.T, up_weight.T
    far_w = core_swap(
        jnp.stack(
            [
                lax.dynamic_slice_in_dim(w, (2 * f + 1 - c) * quarter, quarter, 1)
                for f in range(2)
                for w in (gate_t, up_t)
            ]
        )
    )

    error = jnp.pad(lax.dynamic_slice_in_dim(weight_error, z * n, n, 1), ((0, 0), (0, 128 - n)))
    half = width // 2
    wh_own, wh_sent = (
        jnp.dot(
            weight_error,
            lax.dynamic_slice_in_dim(hessian_slab, core * half, half, 1),
            precision=lax.Precision.HIGH,
            preferred_element_type=F32,
        )
        for core in (c, 1 - c)
    )
    b0, wh_own, wh_sent, far_w, high, low = lax.optimization_barrier(
        (b0, wh_own, wh_sent, far_w, *split_bf16(error))
    )

    b1 = plane_permute(b0, 0, 1)
    b3 = plane_permute(b0, 0, 3)
    b2 = plane_permute(b0, 0, 2)
    weights = weights_call(pos, gate_t, up_t, far_w.reshape(2, 2, n, quarter))
    sb = jnp.concatenate([b1, b3], 0)
    s3b = plane_permute(sb, 1, 3)
    s1b = plane_permute(sb, 1, 1)
    sa = jnp.concatenate([b0, b2], 0)
    s1a = plane_permute(sa, 1, 1)
    s3a = plane_permute(sa, 1, 3)
    s2b = plane_permute(s3b, 1, 1)
    s2a = plane_permute(s1a, 1, 3)
    wh_far = core_swap(wh_sent)
    wh = (wh_own + wh_far).astype(BF16)
    own, far = [], []
    for buffer, f in zip((sa, sb, s1a, s1b, s3a, s3b, s2a, s2b), (0, 1 - c, c, 1, c, 1, 0, 1 - c)):
        mine, theirs = products(buffer, weights, f)
        own.append(mine)
        far.append(theirs)
    far = [jnp.concatenate(part, 0) for part in (far[:6], far[6:])]
    far = [core_swap(part) for part in far]
    sent, hidden_t = activate_call(pos, own, far, (high, low), wh, n)

    f1, g1 = shift_z(hidden_t, 1), shift_z(hidden_t, -1)
    f2, g2 = shift_z(f1, 1), shift_z(g1, -1)
    arrived = exchange(sent, CAL_GR)
    arrived, f2, g2 = lax.optimization_barrier((arrived, f2, g2))
    f3, g3 = shift_z(f2, 1), shift_z(g2, -1)
    panel_width = 8 * n
    starts = slab_offset[0] + jnp.arange(8, dtype=jnp.int32) * width
    wanted = choose_call(jnp.minimum(starts // panel_width, 29), arrived)
    pieces = exchange(wanted, "gc")
    sums = jnp.sum(arrived[:, :, 640:].reshape(16, 2, 16, half).astype(F32), axis=0)
    wh = jnp.concatenate([sums[0], sums[1]], 1)
    pieces, f3, g3, wh = lax.optimization_barrier((pieces, f3, g3, wh))
    f4, g4 = shift_z(f3[:64], 1), shift_z(g3[64:], -1)
    h4 = jnp.concatenate([f4, g4], 0)
    start = slab_offset[0] + z * width
    shift = start - jnp.minimum(start // panel_width, 29) * panel_width
    chunk, total = assemble_call(pieces, jnp.stack([shift, c]).astype(jnp.int32), width, n)
    near = exchange(chunk, PLANE).reshape(256, width)
    return slab_call(
        pos, token_count, (hidden_t, f1, g1, f2, g2, f3, g3, h4), near, core_swap(near), total, wh, hessian_slab
    )


def solution(mesh):
    split = Mesh(
        mesh.devices.reshape(mesh.shape["cal"], 2, 4, 2, mesh.shape["gc"]),
        ("cal", "gr_0", "gr_1", "gr_2", "gc"),
    )

    return jax.shard_map(
        on_device,
        mesh=split,
        in_specs=(
            P(GR_GC, "cal"),
            P(None, CAL_GR_GC),
            P(None, CAL_GR_GC),
            P(CAL_GR, "gc"),
            P(None, CAL_GR),
            P(),
            P(),
        ),
        out_specs=(P(CAL_GR, "gc"), P(CAL_GR, "gc")),
        check_vma=False,
    )
```

```python
import jax
import jax.numpy as jnp
from jax import lax
from jax.experimental import pallas as pl
from jax.experimental.pallas import tpu as pltpu
from jax.sharding import Mesh
from jax.sharding import PartitionSpec as P

GR_GC = ("gr_0", "gr_1", "gr_2", "gc")
PLANE = ("cal", "gr_0", "gr_1")
CAL_GR = ("cal", "gr_0", "gr_1", "gr_2")
CAL_GR_GC = ("cal", "gr_0", "gr_1", "gr_2", "gc")


F32 = jnp.float32
BF16 = jnp.bfloat16
NT = (((1,), (1,)), ((), ()))
VMEM = pl.BlockSpec(memory_space=pltpu.VMEM)
SMEM = pl.BlockSpec(memory_space=pltpu.SMEM)


def plane_index(x, y, c):
    return (((x & 1) * 2 + (x >> 1)) * 4 + y) * 2 + c


def plane_permute(array, on_x_of_core, k):
    pairs = []
    for x in range(4):
        for y in range(4):
            for c in range(2):
                to = (x ^ k, y) if c == on_x_of_core else (x, y ^ k)
                pairs.append((plane_index(x, y, c), plane_index(*to, c)))
    return lax.ppermute(array, CAL_GR, pairs)


def core_swap(array):
    return lax.ppermute(array, "gr_2", [(0, 1), (1, 0)])


def shift_z(array, d):
    return lax.ppermute(array, "gc", [(i, (i + d) % 8) for i in range(8)])


def swap_z(array, k):
    return lax.ppermute(array, "gc", [(i, i ^ k) for i in range(8)])


def exchange(array, axes):
    return lax.all_to_all(array, axes, split_axis=0, concat_axis=0, tiled=True)


def split_bf16(a):
    high = a.astype(BF16)
    return high, (a - high.astype(F32)).astype(BF16)


GROUPS = ((0, 0), (0, 1), (1, 0), (1, 1), (3, 0), (3, 1), (2, 0), (2, 1))


def weights_kernel(pos_ref, gate, up, far, out_ref):
    n = gate.shape[0]
    for i, part in enumerate((gate[...], up[...], far[0, 0], far[0, 1])):
        out_ref[0, i * 128 : i * 128 + n, :] = part
        out_ref[0, i * 128 + n : (i + 1) * 128, :] = jnp.zeros((128 - n, part.shape[1]), BF16)


def weights_call(pos, gate_t, up_t, far_w):
    n, depth = far_w.shape[2:]
    columns = pl.BlockSpec((n, depth), lambda f, pos: (0, (f ^ pos[0]) * 2 + pos[3]))
    return pl.pallas_call(
        weights_kernel,
        grid_spec=pltpu.PrefetchScalarGridSpec(
            num_scalar_prefetch=1,
            grid=(2,),
            in_specs=[columns, columns, pl.BlockSpec((1, 2, n, depth), lambda f, pos: (f ^ pos[0], 0, 0, 0))],
            out_specs=pl.BlockSpec((1, 512, depth), lambda f, pos: (f, 0, 0)),
        ),
        out_shape=jax.ShapeDtypeStruct((2, 512, depth), BF16),
        compiler_params=pltpu.CompilerParams(vmem_limit_bytes=12 << 20),
        name="weights",
    )(pos, gate_t, up_t, far_w)


def products(tokens, weights, f):
    w = weights[f] if isinstance(f, int) else lax.dynamic_index_in_dim(weights, f, 0, keepdims=False)
    return [lax.dot_general(tokens, half, NT, preferred_element_type=F32) for half in (w[:256], w[256:])]


def activate(pos_ref, *refs):
    own, far = refs[:8], refs[8:10]
    high_ref, low_ref, wh_ref, out_ref, ht_ref, sum_ref = refs[10:]
    c = pos_ref[3]
    xh, y = pos_ref[1], pos_ref[2]
    sum_ref[...] = jnp.zeros_like(sum_ref)
    for i, (m, g) in enumerate(GROUPS):
        theirs = far[0][i * 128 : (i + 1) * 128, :] if i < 6 else far[1][(i - 6) * 128 : (i - 5) * 128, :]
        for core, part in ((c, own[i][...]), (1 - c, theirs)):
            for j in range(2):
                block = jnp.where(
                    core == 0,
                    (xh ^ j) * 4 + (y ^ m),
                    (xh ^ (m >> 1)) * 4 + (y ^ (g + 2 * j)),
                )
                at = pl.ds(pl.multiple_of(block * 64, 64), 64)
                sum_ref[at, :] += part[j * 64 : (j + 1) * 64]
    both = sum_ref[...]
    gate, up = both[:, :128], both[:, 128:]
    hidden = gate / (1.0 + jnp.exp(-gate)) * up
    low = hidden.astype(BF16)
    for q in range(32):
        chunk = (q & 1) * 16 + (q >> 1)
        out_ref[q, :, :128] = low[chunk * 16 : (chunk + 1) * 16, :]
    n = ht_ref.shape[0]
    for half in range(2):
        at = pl.ds(pl.multiple_of((half ^ c) * 256, 256), 256)
        ht_ref[:, at] = hidden[half * 256 : (half + 1) * 256, :].T[:n].astype(BF16)
    part = lax.dot_general(high_ref[...], low, NT, preferred_element_type=F32)
    part += lax.dot_general(low_ref[...], low, NT, preferred_element_type=F32)
    part = part.astype(BF16)
    for q in range(32):
        out_ref[q, :, 128:640] = part[q * 16 : (q + 1) * 16, :]
        out_ref[q, :, 640:] = wh_ref[q * 16 : (q + 1) * 16, :]


def activate_call(pos, own, far, error, wh, n):
    return pl.pallas_call(
        activate,
        out_shape=(
            jax.ShapeDtypeStruct((32, 16, 640 + wh.shape[1]), BF16),
            jax.ShapeDtypeStruct((n, 512), BF16),
        ),
        in_specs=[SMEM] + [VMEM] * 13,
        out_specs=(VMEM, VMEM),
        scratch_shapes=[pltpu.VMEM((512, 256), F32)],
        compiler_params=pltpu.CompilerParams(vmem_limit_bytes=12 << 20),
        name="activate",
    )(pos, *own, *far, *error, wh)


def choose(first_ref, arrived_ref, out_ref, total_ref):
    for k in range(8):
        for p in range(3):
            out_ref[k, :, p * 128 : (p + 1) * 128] = arrived_ref[first_ref[k] + p, :, :128]
    total_ref[...] = jnp.sum(arrived_ref[:, :, 128:].astype(F32), axis=0)


def choose_call(first, arrived):
    return pl.pallas_call(
        choose,
        grid_spec=pltpu.PrefetchScalarGridSpec(
            num_scalar_prefetch=1,
            grid=(1,),
            in_specs=[pl.BlockSpec((32, 16, 640), lambda i, first: (0, 0, 0))],
            out_specs=(
                pl.BlockSpec((8, 16, 384), lambda i, first: (0, 0, 0)),
                pl.BlockSpec((16, 512), lambda i, first: (0, 0)),
            ),
        ),
        out_shape=(
            jax.ShapeDtypeStruct((8, 16, 384), BF16),
            jax.ShapeDtypeStruct((16, 512), F32),
        ),
        compiler_params=pltpu.CompilerParams(vmem_limit_bytes=6 << 20),
        name="choose",
    )(first, arrived)


def assemble(n, shift_ref, y_ref, chunk_ref, line_ref):
    for p in range(3):
        for z in range(8):
            line_ref[:, pl.ds((p * 8 + z) * n, n)] = y_ref[z, :, p * 128 : p * 128 + n].astype(F32)
    width = chunk_ref.shape[2]
    d = shift_ref[0]
    base = pl.multiple_of((d // 128) * 128, 128)
    near = line_ref[:, pl.ds(base, width + 128)]
    turned = pltpu.roll(near, width + 128 - (d - base), 1)
    chunk = turned[:, :width].astype(BF16)
    for k in range(chunk_ref.shape[0]):
        chunk_ref[k] = chunk


def assemble_call(pieces, shift, width, n):
    def kernel(*refs):
        assemble(n, *refs)

    return pl.pallas_call(
        kernel,
        out_shape=jax.ShapeDtypeStruct((16, 16, width), BF16),
        in_specs=[SMEM, VMEM],
        out_specs=VMEM,
        scratch_shapes=[pltpu.VMEM((16, 24 * n), F32)],
        compiler_params=pltpu.CompilerParams(vmem_limit_bytes=6 << 20),
        name="assemble",
    )(shift, pieces)


def slab_kernel(pos_ref, count_ref, *refs):
    pieces = refs[:8]
    near, far, total_ref, wh_ref, slab_ref, new_ref, grad_ref, panel_ref = refs[8:]
    z = pos_ref[4]
    n = pieces[0].shape[0]

    @pl.when(pl.program_id(0) == 0)
    def _():
        for piece, d in zip(pieces, (0, -1, 1, -2, 2, -3, 3, 4)):
            at = pl.multiple_of(((z + d + 8) % 8) * n, 16)
            panel_ref[pl.ds(at, piece.shape[0]), :] = piece[...]

    scale = 1.0 / jnp.full((1, 1), count_ref[0].astype(F32), F32)
    gram = jnp.dot(panel_ref[:, :256], near[...], preferred_element_type=F32)
    gram += jnp.dot(panel_ref[:, 256:], far[...], preferred_element_type=F32)
    new_ref[...] = slab_ref[...] + gram * scale
    added = jnp.zeros_like(grad_ref)
    for half, rows in ((pos_ref[3], near), (1 - pos_ref[3], far)):
        part = total_ref[:, pl.ds(pl.multiple_of(half * 256, 256), 256)]
        for term in split_bf16(part):
            added += jnp.dot(term, rows[...], preferred_element_type=F32)
    grad_ref[...] = wh_ref[...] + added * scale


def slab_call(pos, count, pieces, near, far, total, wh, slab):
    rows, width = slab.shape
    step = 512

    def fixed(a):
        return pl.BlockSpec(a.shape, lambda k, *_: (0,) * a.ndim)

    def columns(r):
        return pl.BlockSpec((r, step), lambda k, *_: (0, k))

    return pl.pallas_call(
        slab_kernel,
        grid_spec=pltpu.PrefetchScalarGridSpec(
            num_scalar_prefetch=2,
            grid=(width // step,),
            in_specs=[fixed(p) for p in pieces]
            + [columns(256), columns(256), fixed(total), columns(16), columns(rows)],
            out_specs=(columns(rows), columns(16)),
            scratch_shapes=[pltpu.VMEM((rows, 512), BF16)],
        ),
        out_shape=(
            jax.ShapeDtypeStruct((rows, width), F32),
            jax.ShapeDtypeStruct((16, width), F32),
        ),
        compiler_params=pltpu.CompilerParams(vmem_limit_bytes=20 << 20),
        name="slab",
    )(pos, count, *pieces, near, far, total, wh, slab)


def on_device(tokens, gate_weight, up_weight, hessian_slab, weight_error, slab_offset, token_count):
    xl, xh, y, c, z = (lax.axis_index(a) for a in CAL_GR_GC)
    pos = jnp.stack([xl, xh, y, c, z]).astype(jnp.int32)
    n = gate_weight.shape[1]
    width = hessian_slab.shape[1]
    quarter = tokens.shape[1] // 2

    mine = lax.dynamic_slice_in_dim(tokens, c * quarter, quarter, 1)
    theirs = core_swap(lax.dynamic_slice_in_dim(tokens, (1 - c) * quarter, quarter, 1))
    piece = jnp.concatenate([jnp.where(c == 0, mine, theirs), jnp.where(c == 0, theirs, mine)], 0)
    copies = jnp.broadcast_to(piece[None], (8, *piece.shape))
    copies, gate_weight, up_weight, weight_error = lax.optimization_barrier(
        (copies, gate_weight, up_weight, weight_error)
    )
    b0 = exchange(copies, "gc").reshape(64, quarter)
    gate_t, up_t = gate_weight.T, up_weight.T
    far_w = core_swap(
        jnp.stack(
            [
                lax.dynamic_slice_in_dim(w, (2 * f + 1 - c) * quarter, quarter, 1)
                for f in range(2)
                for w in (gate_t, up_t)
            ]
        )
    )

    error = jnp.pad(lax.dynamic_slice_in_dim(weight_error, z * n, n, 1), ((0, 0), (0, 128 - n)))
    half = width // 2
    wh_own, wh_sent = (
        jnp.dot(
            weight_error,
            lax.dynamic_slice_in_dim(hessian_slab, core * half, half, 1),
            precision=lax.Precision.HIGH,
            preferred_element_type=F32,
        )
        for core in (c, 1 - c)
    )
    b0, wh_own, wh_sent, far_w, high, low = lax.optimization_barrier(
        (b0, wh_own, wh_sent, far_w, *split_bf16(error))
    )

    b1 = plane_permute(b0, 0, 1)
    b3 = plane_permute(b0, 0, 3)
    b2 = plane_permute(b0, 0, 2)
    weights = weights_call(pos, gate_t, up_t, far_w.reshape(2, 2, n, quarter))
    sb = jnp.concatenate([b1, b3], 0)
    s3b = plane_permute(sb, 1, 3)
    sa = jnp.concatenate([b0, b2], 0)
    s1a = plane_permute(sa, 1, 1)
    s3a = plane_permute(sa, 1, 3)
    s2b = plane_permute(s3b, 1, 1)
    s1b = plane_permute(sb, 1, 1)
    s2a = plane_permute(s1a, 1, 3)
    wh_far = core_swap(wh_sent)
    wh = (wh_own + wh_far).astype(BF16)
    own, far = [], []
    for buffer, f in zip((sa, sb, s1a, s1b, s3a, s3b, s2a, s2b), (0, 1 - c, c, 1, c, 1, 0, 1 - c)):
        mine, theirs = products(buffer, weights, f)
        own.append(mine)
        far.append(theirs)
    far = [jnp.concatenate(part, 0) for part in (far[:6], far[6:])]
    far = [core_swap(part) for part in far]
    sent, hidden_t = activate_call(pos, own, far, (high, low), wh, n)

    f1, g1 = shift_z(hidden_t, 1), shift_z(hidden_t, -1)
    f2, g2 = shift_z(f1, 1), shift_z(g1, -1)
    arrived = exchange(sent, CAL_GR)
    arrived, f2, g2 = lax.optimization_barrier((arrived, f2, g2))
    f3, g3 = shift_z(f2, 1), shift_z(g2, -1)
    panel_width = 8 * n
    starts = slab_offset[0] + jnp.arange(8, dtype=jnp.int32) * width
    wanted, total = choose_call(jnp.minimum(starts // panel_width, 29), arrived)
    pieces = exchange(wanted, "gc")
    sums = jnp.sum(arrived[:, :, 640:].reshape(16, 2, 16, half).astype(F32), axis=0)
    wh = jnp.concatenate([sums[0], sums[1]], 1)
    total += swap_z(total, 1)
    total += swap_z(total, 2)
    pieces, f3, g3, wh, total = lax.optimization_barrier((pieces, f3, g3, wh, total))
    total += swap_z(total, 4)
    f4, g4 = shift_z(f3[:64], 1), shift_z(g3[64:], -1)
    h4 = jnp.concatenate([f4, g4], 0)
    start = slab_offset[0] + z * width
    shift = start - jnp.minimum(start // panel_width, 29) * panel_width
    chunk = assemble_call(pieces, shift.reshape(1).astype(jnp.int32), width, n)
    near = exchange(chunk, PLANE).reshape(256, width)
    near, h4, total = lax.optimization_barrier((near, h4, total))
    return slab_call(
        pos, token_count, (hidden_t, f1, g1, f2, g2, f3, g3, h4), near, core_swap(near), total, wh, hessian_slab
    )


def solution(mesh):
    split = Mesh(
        mesh.devices.reshape(mesh.shape["cal"], 2, 4, 2, mesh.shape["gc"]),
        ("cal", "gr_0", "gr_1", "gr_2", "gc"),
    )

    return jax.shard_map(
        on_device,
        mesh=split,
        in_specs=(
            P(GR_GC, "cal"),
            P(None, CAL_GR_GC),
            P(None, CAL_GR_GC),
            P(CAL_GR, "gc"),
            P(None, CAL_GR),
            P(),
            P(),
        ),
        out_specs=(P(CAL_GR, "gc"), P(CAL_GR, "gc")),
        check_vma=False,
    )
```

```python
import jax
import jax.numpy as jnp
from jax import lax
from jax.experimental import pallas as pl
from jax.experimental.pallas import tpu as pltpu
from jax.sharding import Mesh
from jax.sharding import PartitionSpec as P

GR_GC = ("gr_0", "gr_1", "gr_2", "gc")
PLANE = ("cal", "gr_0", "gr_1")
CAL_GR = ("cal", "gr_0", "gr_1", "gr_2")
CAL_GR_GC = ("cal", "gr_0", "gr_1", "gr_2", "gc")


F32 = jnp.float32
BF16 = jnp.bfloat16
NT = (((1,), (1,)), ((), ()))
VMEM = pl.BlockSpec(memory_space=pltpu.VMEM)
SMEM = pl.BlockSpec(memory_space=pltpu.SMEM)


def plane_index(x, y, c):
    return (((x & 1) * 2 + (x >> 1)) * 4 + y) * 2 + c


def plane_permute(array, on_x_of_core, k):
    pairs = []
    for x in range(4):
        for y in range(4):
            for c in range(2):
                to = (x ^ k, y) if c == on_x_of_core else (x, y ^ k)
                pairs.append((plane_index(x, y, c), plane_index(*to, c)))
    return lax.ppermute(array, CAL_GR, pairs)


def core_swap(array):
    return lax.ppermute(array, "gr_2", [(0, 1), (1, 0)])


def shift_z(array, d):
    return lax.ppermute(array, "gc", [(i, (i + d) % 8) for i in range(8)])


def swap_z(array, k):
    return lax.ppermute(array, "gc", [(i, i ^ k) for i in range(8)])


def exchange(array, axes):
    return lax.all_to_all(array, axes, split_axis=0, concat_axis=0, tiled=True)


def split_bf16(a):
    high = a.astype(BF16)
    return high, (a - high.astype(F32)).astype(BF16)


GROUPS = ((0, 0), (0, 1), (1, 0), (1, 1), (3, 0), (3, 1), (2, 0), (2, 1))


def weights_kernel(pos_ref, gate, up, far, out_ref):
    n = gate.shape[0]
    for i, part in enumerate((gate[...], up[...], far[0, 0], far[0, 1])):
        out_ref[0, i * 128 : i * 128 + n, :] = part
        out_ref[0, i * 128 + n : (i + 1) * 128, :] = jnp.zeros((128 - n, part.shape[1]), BF16)


def weights_call(pos, gate_t, up_t, far_w):
    n, depth = far_w.shape[2:]
    columns = pl.BlockSpec((n, depth), lambda f, pos: (0, (f ^ pos[0]) * 2 + pos[3]))
    return pl.pallas_call(
        weights_kernel,
        grid_spec=pltpu.PrefetchScalarGridSpec(
            num_scalar_prefetch=1,
            grid=(2,),
            in_specs=[columns, columns, pl.BlockSpec((1, 2, n, depth), lambda f, pos: (f ^ pos[0], 0, 0, 0))],
            out_specs=pl.BlockSpec((1, 512, depth), lambda f, pos: (f, 0, 0)),
        ),
        out_shape=jax.ShapeDtypeStruct((2, 512, depth), BF16),
        compiler_params=pltpu.CompilerParams(vmem_limit_bytes=12 << 20),
        name="weights",
    )(pos, gate_t, up_t, far_w)


def products(tokens, weights, f):
    w = weights[f] if isinstance(f, int) else lax.dynamic_index_in_dim(weights, f, 0, keepdims=False)
    return [lax.dot_general(tokens, half, NT, preferred_element_type=F32) for half in (w[:256], w[256:])]


def activate(pos_ref, *refs):
    own, far = refs[:8], refs[8:10]
    high_ref, low_ref, wh_ref, out_ref, ht_ref, sum_ref = refs[10:]
    c = pos_ref[3]
    xh, y = pos_ref[1], pos_ref[2]
    sum_ref[...] = jnp.zeros_like(sum_ref)
    for i, (m, g) in enumerate(GROUPS):
        theirs = far[0][i * 128 : (i + 1) * 128, :] if i < 6 else far[1][(i - 6) * 128 : (i - 5) * 128, :]
        for core, part in ((c, own[i][...]), (1 - c, theirs)):
            for j in range(2):
                block = jnp.where(
                    core == 0,
                    (xh ^ j) * 4 + (y ^ m),
                    (xh ^ (m >> 1)) * 4 + (y ^ (g + 2 * j)),
                )
                at = pl.ds(pl.multiple_of(block * 64, 64), 64)
                sum_ref[at, :] += part[j * 64 : (j + 1) * 64]
    both = sum_ref[...]
    gate, up = both[:, :128], both[:, 128:]
    hidden = gate / (1.0 + jnp.exp(-gate)) * up
    low = hidden.astype(BF16)
    for q in range(32):
        chunk = (q & 1) * 16 + (q >> 1)
        out_ref[q, :, :128] = low[chunk * 16 : (chunk + 1) * 16, :]
    n = ht_ref.shape[0]
    for half in range(2):
        at = pl.ds(pl.multiple_of((half ^ c) * 256, 256), 256)
        ht_ref[:, at] = hidden[half * 256 : (half + 1) * 256, :].T[:n].astype(BF16)
    part = lax.dot_general(high_ref[...], low, NT, preferred_element_type=F32)
    part += lax.dot_general(low_ref[...], low, NT, preferred_element_type=F32)
    part = part.astype(BF16)
    for q in range(32):
        out_ref[q, :, 128:640] = part[q * 16 : (q + 1) * 16, :]
        out_ref[q, :, 640:] = wh_ref[q * 16 : (q + 1) * 16, :]


def activate_call(pos, own, far, error, wh, n):
    return pl.pallas_call(
        activate,
        out_shape=(
            jax.ShapeDtypeStruct((32, 16, 640 + wh.shape[1]), BF16),
            jax.ShapeDtypeStruct((n, 512), BF16),
        ),
        in_specs=[SMEM] + [VMEM] * 13,
        out_specs=(VMEM, VMEM),
        scratch_shapes=[pltpu.VMEM((512, 256), F32)],
        compiler_params=pltpu.CompilerParams(vmem_limit_bytes=12 << 20),
        name="activate",
    )(pos, *own, *far, *error, wh)


def choose(first_ref, arrived_ref, out_ref, total_ref):
    for k in range(8):
        for p in range(3):
            out_ref[k, :, p * 128 : (p + 1) * 128] = arrived_ref[first_ref[k] + p, :, :128]
    total_ref[...] = jnp.sum(arrived_ref[:, :, 128:].astype(F32), axis=0)


def choose_call(first, arrived):
    return pl.pallas_call(
        choose,
        grid_spec=pltpu.PrefetchScalarGridSpec(
            num_scalar_prefetch=1,
            grid=(1,),
            in_specs=[pl.BlockSpec((32, 16, 640), lambda i, first: (0, 0, 0))],
            out_specs=(
                pl.BlockSpec((8, 16, 384), lambda i, first: (0, 0, 0)),
                pl.BlockSpec((16, 512), lambda i, first: (0, 0)),
            ),
        ),
        out_shape=(
            jax.ShapeDtypeStruct((8, 16, 384), BF16),
            jax.ShapeDtypeStruct((16, 512), F32),
        ),
        compiler_params=pltpu.CompilerParams(vmem_limit_bytes=6 << 20),
        name="choose",
    )(first, arrived)


def assemble(n, shift_ref, y_ref, chunk_ref, line_ref):
    for p in range(3):
        for z in range(8):
            line_ref[:, pl.ds((p * 8 + z) * n, n)] = y_ref[z, :, p * 128 : p * 128 + n].astype(F32)
    width = chunk_ref.shape[2]
    d = shift_ref[0]
    base = pl.multiple_of((d // 128) * 128, 128)
    near = line_ref[:, pl.ds(base, width + 128)]
    turned = pltpu.roll(near, width + 128 - (d - base), 1)
    chunk = turned[:, :width].astype(BF16)
    for k in range(chunk_ref.shape[0]):
        chunk_ref[k] = chunk


def assemble_call(pieces, shift, width, n):
    def kernel(*refs):
        assemble(n, *refs)

    return pl.pallas_call(
        kernel,
        out_shape=jax.ShapeDtypeStruct((16, 16, width), BF16),
        in_specs=[SMEM, VMEM],
        out_specs=VMEM,
        scratch_shapes=[pltpu.VMEM((16, 24 * n), F32)],
        compiler_params=pltpu.CompilerParams(vmem_limit_bytes=6 << 20),
        name="assemble",
    )(shift, pieces)


def slab_kernel(pos_ref, count_ref, *refs):
    pieces = refs[:8]
    near, far, total_ref, wh_ref, slab_ref, new_ref, grad_ref, panel_ref, old_ref, sems = refs[8:]
    z = pos_ref[4]
    n = pieces[0].shape[0]

    steps, _, step = old_ref.shape
    copies = [
        pltpu.make_async_copy(slab_ref.at[:, k * step : (k + 1) * step], old_ref.at[k], sems.at[k])
        for k in range(steps)
    ]

    @pl.when(pl.program_id(0) == 0)
    def _():
        for copy in copies:
            copy.start()
        for piece, d in zip(pieces, (0, -1, 1, -2, 2, -3, 3, 4)):
            at = pl.multiple_of(((z + d + 8) % 8) * n, 16)
            panel_ref[pl.ds(at, piece.shape[0]), :] = piece[...]

    scale = 1.0 / jnp.full((1, 1), count_ref[0].astype(F32), F32)
    gram = jnp.dot(panel_ref[:, :256], near[...], preferred_element_type=F32)
    gram += jnp.dot(panel_ref[:, 256:], far[...], preferred_element_type=F32)
    for k, copy in enumerate(copies):

        @pl.when(pl.program_id(0) == k)
        def _(k=k, copy=copy):
            copy.wait()
            new_ref[...] = old_ref[k] + gram * scale

    added = jnp.zeros_like(grad_ref)
    for half, rows in ((pos_ref[3], near), (1 - pos_ref[3], far)):
        part = total_ref[:, pl.ds(pl.multiple_of(half * 256, 256), 256)]
        for term in split_bf16(part):
            added += jnp.dot(term, rows[...], preferred_element_type=F32)
    grad_ref[...] = wh_ref[...] + added * scale


def slab_call(pos, count, pieces, near, far, total, wh, slab):
    rows, width = slab.shape
    step = 256

    def fixed(a):
        return pl.BlockSpec(a.shape, lambda k, *_: (0,) * a.ndim)

    def columns(r):
        return pl.BlockSpec((r, step), lambda k, *_: (0, k))

    return pl.pallas_call(
        slab_kernel,
        grid_spec=pltpu.PrefetchScalarGridSpec(
            num_scalar_prefetch=2,
            grid=(width // step,),
            in_specs=[fixed(p) for p in pieces]
            + [columns(256), columns(256), fixed(total), columns(16)]
            + [pl.BlockSpec(memory_space=pltpu.HBM)],
            out_specs=(columns(rows), columns(16)),
            scratch_shapes=[
                pltpu.VMEM((rows, 512), BF16),
                pltpu.VMEM((width // step, rows, step), F32),
                pltpu.SemaphoreType.DMA((width // step,)),
            ],
        ),
        out_shape=(
            jax.ShapeDtypeStruct((rows, width), F32),
            jax.ShapeDtypeStruct((16, width), F32),
        ),
        compiler_params=pltpu.CompilerParams(vmem_limit_bytes=50 << 20),
        name="slab",
    )(pos, count, *pieces, near, far, total, wh, slab)


def on_device(tokens, gate_weight, up_weight, hessian_slab, weight_error, slab_offset, token_count):
    xl, xh, y, c, z = (lax.axis_index(a) for a in CAL_GR_GC)
    pos = jnp.stack([xl, xh, y, c, z]).astype(jnp.int32)
    n = gate_weight.shape[1]
    width = hessian_slab.shape[1]
    quarter = tokens.shape[1] // 2

    mine = lax.dynamic_slice_in_dim(tokens, c * quarter, quarter, 1)
    theirs = core_swap(lax.dynamic_slice_in_dim(tokens, (1 - c) * quarter, quarter, 1))
    piece = jnp.concatenate([jnp.where(c == 0, mine, theirs), jnp.where(c == 0, theirs, mine)], 0)
    copies = jnp.broadcast_to(piece[None], (8, *piece.shape))
    copies, gate_weight, up_weight, weight_error = lax.optimization_barrier(
        (copies, gate_weight, up_weight, weight_error)
    )
    b0 = exchange(copies, "gc").reshape(64, quarter)
    gate_t, up_t = gate_weight.T, up_weight.T
    far_w = core_swap(
        jnp.stack(
            [
                lax.dynamic_slice_in_dim(w, (2 * f + 1 - c) * quarter, quarter, 1)
                for f in range(2)
                for w in (gate_t, up_t)
            ]
        )
    )

    error = jnp.pad(lax.dynamic_slice_in_dim(weight_error, z * n, n, 1), ((0, 0), (0, 128 - n)))
    half = width // 2
    wh_own, wh_sent = (
        jnp.dot(
            weight_error,
            lax.dynamic_slice_in_dim(hessian_slab, core * half, half, 1),
            precision=lax.Precision.HIGH,
            preferred_element_type=F32,
        )
        for core in (c, 1 - c)
    )
    b0, wh_own, wh_sent, far_w, high, low = lax.optimization_barrier(
        (b0, wh_own, wh_sent, far_w, *split_bf16(error))
    )

    b1 = plane_permute(b0, 0, 1)
    b3 = plane_permute(b0, 0, 3)
    b2 = plane_permute(b0, 0, 2)
    weights = weights_call(pos, gate_t, up_t, far_w.reshape(2, 2, n, quarter))
    sb = jnp.concatenate([b1, b3], 0)
    s3b = plane_permute(sb, 1, 3)
    sa = jnp.concatenate([b0, b2], 0)
    s1a = plane_permute(sa, 1, 1)
    s3a = plane_permute(sa, 1, 3)
    s2b = plane_permute(s3b, 1, 1)
    s1b = plane_permute(sb, 1, 1)
    s2a = plane_permute(s1a, 1, 3)
    wh_far = core_swap(wh_sent)
    wh = (wh_own + wh_far).astype(BF16)
    own, far = [], []
    for buffer, f in zip((sa, sb, s1a, s1b, s3a, s3b, s2a, s2b), (0, 1 - c, c, 1, c, 1, 0, 1 - c)):
        mine, theirs = products(buffer, weights, f)
        own.append(mine)
        far.append(theirs)
    far = [jnp.concatenate(part, 0) for part in (far[:6], far[6:])]
    far = [core_swap(part) for part in far]
    sent, hidden_t = activate_call(pos, own, far, (high, low), wh, n)

    f1, g1 = shift_z(hidden_t, 1), shift_z(hidden_t, -1)
    f2, g2 = shift_z(f1, 1), shift_z(g1, -1)
    arrived = exchange(sent, CAL_GR)
    arrived, f2, g2 = lax.optimization_barrier((arrived, f2, g2))
    f3, g3 = shift_z(f2, 1), shift_z(g2, -1)
    panel_width = 8 * n
    starts = slab_offset[0] + jnp.arange(8, dtype=jnp.int32) * width
    wanted, total = choose_call(jnp.minimum(starts // panel_width, 29), arrived)
    pieces = exchange(wanted, "gc")
    sums = jnp.sum(arrived[:, :, 640:].reshape(16, 2, 16, half).astype(F32), axis=0)
    wh = jnp.concatenate([sums[0], sums[1]], 1)
    total += swap_z(total, 1)
    total += swap_z(total, 2)
    total += swap_z(total, 4)
    f4, g4 = shift_z(f3[:64], 1), shift_z(g3[64:], -1)
    h4 = jnp.concatenate([f4, g4], 0)
    start = slab_offset[0] + z * width
    shift = start - jnp.minimum(start // panel_width, 29) * panel_width
    chunk = assemble_call(pieces, shift.reshape(1).astype(jnp.int32), width, n)
    near = exchange(chunk, PLANE).reshape(256, width)
    near, h4, total = lax.optimization_barrier((near, h4, total))
    return slab_call(
        pos, token_count, (hidden_t, f1, g1, f2, g2, f3, g3, h4), near, core_swap(near), total, wh, hessian_slab
    )


def solution(mesh):
    split = Mesh(
        mesh.devices.reshape(mesh.shape["cal"], 2, 4, 2, mesh.shape["gc"]),
        ("cal", "gr_0", "gr_1", "gr_2", "gc"),
    )

    return jax.shard_map(
        on_device,
        mesh=split,
        in_specs=(
            P(GR_GC, "cal"),
            P(None, CAL_GR_GC),
            P(None, CAL_GR_GC),
            P(CAL_GR, "gc"),
            P(None, CAL_GR),
            P(),
            P(),
        ),
        out_specs=(P(CAL_GR, "gc"), P(CAL_GR, "gc")),
        check_vma=False,
    )
```
